32 devices in a mesh: seq: 8 (over z, y), samp: 4 (over x, core).
Axes of the slice: x: 2, y: 2, z: 4, core: 2. Of those that a mesh axis runs over, the one named last changes fastest.
Arguments:
- atoms: bfloat16 [48, 4096, 128], P('samp', 'seq'), may hold values from -3 to 3
- gain: float32 [128], replicated, may hold values from 0.25 to 1.75
- w_query: bfloat16 [128, 128], replicated, may hold values from -0.5 to 0.5
- w_key: bfloat16 [128, 128], replicated, may hold values from -0.5 to 0.5
- w_value: bfloat16 [128, 128], replicated, may hold values from -0.5 to 0.5
- w_gate: bfloat16 [128, 128], replicated, may hold values from -0.5 to 0.5
- w_out: bfloat16 [128, 128], replicated, may hold values from -0.5 to 0.5
- w_token: bfloat16 [128, 768], replicated, may hold values from -0.5 to 0.5
- w_pair: bfloat16 [16, 4], replicated, may hold values from -1.5 to 1.5
- pair_cond: bfloat16 [128, 32, 2048], P('seq'), may hold values from -6 to 6
- counts: int32 [8], replicated, may hold values from 472 to 512, as said below
- membership: int32 [4096], P('seq'), may hold values from 0 to 383, as said below
- pooled_cot: bfloat16 [48, 384, 768], P('samp', 'seq'), may hold values from -6 to 6
Outputs:
- pooled: bfloat16 [48, 384, 768], P('samp', 'seq')
- grad_atoms: bfloat16 [48, 4096, 128], P('samp', 'seq')
- grad_gain: float32 [128], replicated
- grad_query: float32 [128, 128], replicated
- grad_key: float32 [128, 128], replicated
- grad_value: float32 [128, 128], replicated
- grad_gate: float32 [128, 128], replicated
- grad_out: float32 [128, 128], replicated
- grad_token: float32 [128, 768], replicated
- grad_pair: float32 [16, 4], replicated
The draws below stay inside these ranges and needn't reach their ends.
Inputs may be any that keep to these rules, and one draw needn't show every extreme that they name: `counts`: live atoms fill the first slots of each shard; some shard is full. `membership`: slots of shard s name tokens s * 48 to (s + 1) * 48 - 1, never falling along the slots; every token has one or more live atoms; slots past the shard's count name its last token.
All inputs are finite; a program needn't handle non-finite values.
Results may differ from the reference program's by a relative error of at most 0.012.
Values may be sent and summed in bfloat16 or wider, within the bound.
A program may use at most 128 MiB of HBM per device.

```python
import jax
import jax.numpy as jnp
from jax import lax

D = 128
HEADS = 4
CP = 16
TOKW = 768
QBLK = 32
KWIN = 128
ATOM_DEV = 512
TOK_DEV = 48
ATOMS = 4096
TOKENS = 384
SAMPLES = 48
N_SEQ = 8


def shard_counts(key):
    base_key = jax.random.fold_in(key, 11)
    drawn_counts = jax.random.randint(jax.random.fold_in(base_key, 1), (N_SEQ,), ATOM_DEV - 40, ATOM_DEV + 1)
    fullest = jax.random.randint(jax.random.fold_in(base_key, 2), (), 0, N_SEQ)
    return jnp.where(jnp.arange(N_SEQ) == fullest, ATOM_DEV, drawn_counts).astype(jnp.int32)


def draw_counts(key, part):
    return shard_counts(key)


def draw_membership(key, part):
    counts = shard_counts(key)
    base_key = jax.random.fold_in(key, 23)
    slot_ids = jnp.arange(ATOM_DEV, dtype=jnp.int32)

    def one_shard(shard_index):
        extra_ids = jax.random.randint(jax.random.fold_in(base_key, shard_index), (ATOM_DEV,), 0, TOK_DEV).astype(jnp.int32)
        values = jnp.where(slot_ids < TOK_DEV, slot_ids, extra_ids)
        values = jnp.where(slot_ids < counts[shard_index], values, TOK_DEV)
        ordered = jnp.minimum(jnp.sort(values), TOK_DEV - 1)
        return ordered + shard_index * TOK_DEV
    return jax.vmap(one_shard)(jnp.arange(N_SEQ, dtype=jnp.int32)).reshape(-1).astype(jnp.int32)


def levels(key, dims, split, smallest, top_value):
    loudness = 1.0
    for axis_at, parts in split:
        steps = jax.random.uniform(jax.random.fold_in(jax.random.fold_in(key, 6), axis_at), (parts,), jnp.float32, smallest / len(split), top_value / len(split))
        loudness = loudness * jnp.repeat(jnp.exp(steps), dims[axis_at] // parts).reshape((-1,) + (1,) * (len(dims) - 1 - axis_at))
    return loudness


def bell_draw(stream_key, shape, scale, limit, cuts=(), held_as=jnp.bfloat16):
    values = jax.random.normal(stream_key, shape, jnp.float32) * scale
    if len(cuts) > 0:
        values = levels(stream_key, shape, cuts, -0.22, 0.18) * values
    return jnp.clip(values, min=-limit, max=limit).astype(held_as)


def setup_inputs(seed: int = 0) -> dict:
    key_list = jax.random.split(jax.random.key(seed), 14)
    atoms = bell_draw(key_list[0], (SAMPLES, ATOMS, D), 0.5, 3.0, ((0, 4), (1, 8)))
    gain = jnp.clip(1.0 + 0.15 * jax.random.normal(key_list[1], (D,), jnp.float32), 0.25, 1.75)
    w_query = bell_draw(key_list[2], (D, D), D ** -0.5, 0.5)
    w_key = bell_draw(key_list[3], (D, D), D ** -0.5, 0.5)
    w_value = bell_draw(key_list[4], (D, D), D ** -0.5, 0.5)
    w_gate = bell_draw(key_list[5], (D, D), D ** -0.5, 0.5)
    w_out = bell_draw(key_list[6], (D, D), D ** -0.5, 0.5)
    w_token = bell_draw(key_list[7], (D, TOKW), D ** -0.5, 0.5)
    w_pair = bell_draw(key_list[8], (CP, HEADS), CP ** -0.5, 1.5)
    pair_cond = bell_draw(key_list[9], (ATOMS // QBLK, QBLK, KWIN * CP), 1.0, 6.0, ((0, 8),))
    counts = draw_counts(jax.random.fold_in(key_list[13], 71), 0)
    membership = draw_membership(jax.random.fold_in(key_list[13], 71), 0)
    pooled_cot = bell_draw(key_list[12], (SAMPLES, TOKENS, TOKW), 1.0, 6.0, ((0, 4), (1, 8)))
    return {"atoms": atoms, "gain": gain, "w_query": w_query, "w_key": w_key, "w_value": w_value, "w_gate": w_gate, "w_out": w_out, "w_token": w_token, "w_pair": w_pair, "pair_cond": pair_cond, "counts": counts, "membership": membership, "pooled_cot": pooled_cot}


epsilon = 1e-05
highest = lax.Precision.HIGHEST

def windows(extended, blocks):
    span_blocks = KWIN // QBLK
    blocked = extended.reshape((blocks + span_blocks - 1, QBLK) + extended.shape[1:])
    return jnp.concatenate([blocked[offset:offset + blocks] for offset in range(span_blocks)], axis=1)

def unwindow(grad_windows, blocks):
    span_blocks = KWIN // QBLK
    summed = None
    for offset in range(span_blocks):
        grad_piece = grad_windows[:, offset * QBLK:(offset + 1) * QBLK]
        pad_widths = [(offset, span_blocks - 1 - offset)] + [(0, 0)] * (grad_piece.ndim - 1)
        padded = jnp.pad(grad_piece, pad_widths)
        summed = padded if summed is None else summed + padded
    return summed.reshape((QBLK * (blocks + span_blocks - 1),) + grad_windows.shape[2:])

def rounded(value):
    return lax.optimization_barrier(value.astype(jnp.bfloat16)).astype(jnp.float32)

def sample_pass(atoms, queries, keys_ext, values_ext, gate_pre, key_mask, pair_bias, w_out, w_token, member, inv_count, cotangent):
    atom_rows, model_width = atoms.shape
    blocks = atom_rows // QBLK
    head_dim = model_width // HEADS
    scaling = head_dim ** (-0.5)
    query_heads = queries.reshape(blocks, QBLK, HEADS, head_dim).astype(jnp.float32)
    key_heads = windows(keys_ext, blocks).reshape(blocks, KWIN, HEADS, head_dim).astype(jnp.float32)
    value_heads = windows(values_ext, blocks).reshape(blocks, KWIN, HEADS, head_dim).astype(jnp.float32)
    scores = jnp.einsum('bihd,bjhd->bhij', query_heads, key_heads) * scaling + pair_bias
    exp_scores = jnp.where(key_mask[:, None, None, :], jnp.exp(scores), 0.0)
    attn_probs = exp_scores / lax.optimization_barrier(jnp.sum(exp_scores, axis=-1, keepdims=True))
    probs_low = rounded(attn_probs)
    attended = jnp.einsum('bhij,bjhd->bihd', probs_low, value_heads).reshape(atom_rows, model_width)
    gate_sig = jax.nn.sigmoid(gate_pre)
    gated_out = (gate_sig * attended).astype(jnp.bfloat16)
    updated = (atoms.astype(jnp.float32) + jnp.dot(gated_out, w_out, preferred_element_type=jnp.float32)).astype(jnp.bfloat16)
    token_pre = jnp.dot(updated, w_token, preferred_element_type=jnp.float32)
    token_sig = jax.nn.sigmoid(token_pre)
    token_act = (token_pre * token_sig).astype(jnp.bfloat16)
    shards = member.shape[0]
    channels = token_act.shape[-1]
    grouped = token_act.reshape(shards, -1, channels).astype(jnp.float32)
    member_f = member.astype(jnp.float32)
    pooled = (jnp.einsum('sat,sac->stc', member_f, grouped) * inv_count[:, :, None]).astype(jnp.bfloat16)
    pooled = pooled.reshape(-1, channels)
    scaled_cot = cotangent.reshape(shards, -1, channels).astype(jnp.float32) * inv_count[:, :, None]
    grad_act = jnp.einsum('sat,stc->sac', member_f, scaled_cot, precision=highest).reshape(atom_rows, channels)
    grad_pre = (grad_act * token_sig * (1.0 + token_pre * (1.0 - token_sig))).astype(jnp.bfloat16)
    grad_token = jnp.dot(updated.T, grad_pre, preferred_element_type=jnp.float32)
    grad_updated = jnp.dot(grad_pre, w_token.T, preferred_element_type=jnp.float32).astype(jnp.bfloat16)
    grad_outw = jnp.dot(gated_out.T, grad_updated, preferred_element_type=jnp.float32)
    grad_gated = jnp.dot(grad_updated, w_out.T, preferred_element_type=jnp.float32)
    grad_gatepre = (grad_gated * attended * gate_sig * (1.0 - gate_sig)).astype(jnp.bfloat16)
    grad_att = rounded(grad_gated * gate_sig)
    grad_heads = grad_att.reshape(blocks, QBLK, HEADS, head_dim)
    grad_probs = jnp.einsum('bihd,bjhd->bhij', grad_heads, value_heads)
    grad_scores = attn_probs * (grad_probs - lax.optimization_barrier(jnp.sum(attn_probs * grad_probs, axis=-1, keepdims=True)))
    scores_low = rounded(grad_scores)
    grad_queries = jnp.einsum('bhij,bjhd->bihd', scores_low, key_heads).reshape(atom_rows, model_width) * scaling
    grad_key_win = jnp.einsum('bhij,bihd->bjhd', scores_low, query_heads).reshape(blocks, KWIN, model_width) * scaling
    grad_value_win = jnp.einsum('bhij,bihd->bjhd', probs_low, grad_heads).reshape(blocks, KWIN, model_width)
    return (pooled, grad_updated, grad_queries, unwindow(grad_key_win, blocks), unwindow(grad_value_win, blocks), grad_gatepre, grad_outw, grad_token, grad_scores)

def reference(atoms, gain, w_query, w_key, w_value, w_gate, w_out, w_token, w_pair, pair_cond, counts, membership, pooled_cot):
    rim_width = (KWIN - QBLK) // 2
    blocks = ATOMS // QBLK
    slot_ids = jnp.arange(ATOMS, dtype=jnp.int32)
    alive_slots = slot_ids % ATOM_DEV < counts[slot_ids // ATOM_DEV]
    key_mask = windows(jnp.pad(alive_slots, (rim_width, rim_width)), blocks)
    pair_f = pair_cond.reshape(blocks, QBLK, KWIN, CP).astype(jnp.float32)
    pair_bias = jnp.einsum('bijc,ch->bhij', pair_f, w_pair.astype(jnp.float32))
    local_ids = membership.reshape(N_SEQ, ATOM_DEV) - (jnp.arange(N_SEQ, dtype=jnp.int32) * TOK_DEV)[:, None]
    member = ((local_ids[:, :, None] == jnp.arange(TOK_DEV, dtype=jnp.int32)[None, None, :]) & alive_slots.reshape(N_SEQ, ATOM_DEV)[:, :, None]).astype(jnp.bfloat16)
    inv_count = 1.0 / lax.optimization_barrier(jnp.sum(member.astype(jnp.float32), axis=1))

    def per_sample(totals, inputs):
        sample_atoms, cotangent = inputs
        atoms_f = sample_atoms.astype(jnp.float32)
        centred = atoms_f - lax.optimization_barrier(jnp.mean(atoms_f, axis=-1, keepdims=True))
        variance = lax.optimization_barrier(jnp.mean(centred * centred, axis=-1, keepdims=True))
        inv_std = lax.rsqrt(variance + epsilon)
        normed = centred * inv_std
        hidden = (normed * gain).astype(jnp.bfloat16)
        queries = jnp.dot(hidden, w_query, preferred_element_type=jnp.float32).astype(jnp.bfloat16)
        keys = jnp.dot(hidden, w_key, preferred_element_type=jnp.float32).astype(jnp.bfloat16)
        values = jnp.dot(hidden, w_value, preferred_element_type=jnp.float32).astype(jnp.bfloat16)
        gate_pre = jnp.dot(hidden, w_gate, preferred_element_type=jnp.float32)
        keys_ext = jnp.pad(keys, ((rim_width, rim_width), (0, 0)))
        values_ext = jnp.pad(values, ((rim_width, rim_width), (0, 0)))
        pooled, grad_updated, grad_queries, grad_keys_ext, grad_values_ext, grad_gatepre, grad_outw, grad_tokw, grad_scores = sample_pass(sample_atoms, queries, keys_ext, values_ext, gate_pre, key_mask, pair_bias, w_out, w_token, member, inv_count, cotangent)
        grad_q_low = grad_queries.astype(jnp.bfloat16)
        grad_k_low = grad_keys_ext[rim_width:rim_width + ATOMS].astype(jnp.bfloat16)
        grad_v_low = grad_values_ext[rim_width:rim_width + ATOMS].astype(jnp.bfloat16)
        grad_hidden = jnp.dot(grad_q_low, w_query.T, preferred_element_type=jnp.float32) + jnp.dot(grad_k_low, w_key.T, preferred_element_type=jnp.float32) + jnp.dot(grad_v_low, w_value.T, preferred_element_type=jnp.float32) + jnp.dot(grad_gatepre, w_gate.T, preferred_element_type=jnp.float32)
        grad_normed = grad_hidden * gain
        grad_ln = inv_std * (grad_normed - lax.optimization_barrier(jnp.mean(grad_normed, axis=-1, keepdims=True)) - normed * lax.optimization_barrier(jnp.mean(grad_normed * normed, axis=-1, keepdims=True)))
        grad_sample = (grad_updated.astype(jnp.float32) + grad_ln).astype(jnp.bfloat16)
        acc_gain, acc_query, acc_key, acc_value, acc_gate, acc_out, acc_token, acc_scores = totals
        totals = (acc_gain + lax.optimization_barrier(jnp.sum(grad_hidden * normed, axis=0)), acc_query + jnp.dot(hidden.T, grad_q_low, preferred_element_type=jnp.float32), acc_key + jnp.dot(hidden.T, grad_k_low, preferred_element_type=jnp.float32), acc_value + jnp.dot(hidden.T, grad_v_low, preferred_element_type=jnp.float32), acc_gate + jnp.dot(hidden.T, grad_gatepre, preferred_element_type=jnp.float32), acc_out + grad_outw, acc_token + grad_tokw, acc_scores + grad_scores)
        return (totals, (pooled, grad_sample))
    start = (jnp.zeros((D,), jnp.float32), jnp.zeros((D, D), jnp.float32), jnp.zeros((D, D), jnp.float32), jnp.zeros((D, D), jnp.float32), jnp.zeros((D, D), jnp.float32), jnp.zeros((D, D), jnp.float32), jnp.zeros((D, TOKW), jnp.float32), jnp.zeros((blocks, HEADS, QBLK, KWIN), jnp.float32))
    totals, (pooled, grad_atoms) = lax.scan(per_sample, start, (atoms, pooled_cot))
    grad_gain, grad_query, grad_key, grad_value, grad_gate, grad_out, grad_token, score_sum = totals
    grad_pair = jnp.einsum('bijc,bhij->ch', pair_f, score_sum)
    return (pooled, grad_atoms, grad_gain, grad_query, grad_key, grad_value, grad_gate, grad_out, grad_token, grad_pair)
```

```python
import functools

import jax
import jax.numpy as jnp
from jax import lax
from jax.experimental import pallas as pl
from jax.experimental.pallas import tpu as pltpu
from jax.sharding import PartitionSpec as P

HEADS = 4
QBLK = 32
KWIN = 128
LOG2E = 1.4426950408889634

epsilon = 1e-05
F32 = jnp.float32
BF16 = jnp.bfloat16
NN = (((1,), (0,)), ((), ()))
NT = (((1,), (1,)), ((), ()))
TN = (((0,), (0,)), ((), ()))
GROUP = 4
LANES = 128


def mm(a, b, dims=NN):
    return lax.dot_general(a, b, dims, preferred_element_type=F32)


def sigmoid(x):
    return 0.5 * jnp.tanh(0.5 * x) + 0.5


def layer_norm(x, gain):
    centred = x - jnp.mean(x, axis=-1, keepdims=True)
    variance = jnp.mean(centred * centred, axis=-1, keepdims=True)
    inv_std = lax.rsqrt(variance + epsilon)
    normed = centred * inv_std
    return normed, inv_std, (normed * gain).astype(BF16)


def head_lanes(width):
    lane = lax.broadcasted_iota(jnp.int32, (1, width), 1)
    return lane // (width // HEADS)


def expand(block, masks):
    return jnp.concatenate([block * m for m in masks], axis=0)


def collapse(wide, lane_head):
    rows = wide.shape[0] // HEADS
    out = wide[:rows]
    for h in range(1, HEADS):
        out = jnp.where(lane_head == h, wide[h * rows : (h + 1) * rows], out)
    return out


def lane_swap(parts, lane_block):
    count = len(parts)
    outs = []
    for b in range(count):
        out = None
        for a in range(count):
            shift = (QBLK * (a - b)) % LANES
            moved = parts[a] if shift == 0 else pltpu.roll(parts[a], shift, 1)
            out = moved if out is None else jnp.where(lane_block == a, moved, out)
        outs.append(out)
    return outs


def build_bias(counts_ref, pair_ref, wsm_ref, bias_scr, blocks, rows):
    pos = lax.axis_index("seq")
    size = lax.axis_size("seq")
    own = counts_ref[pos]
    left = jnp.where(pos > 0, counts_ref[jnp.maximum(pos - 1, 0)], 0)
    right = jnp.where(pos < size - 1, counts_ref[jnp.minimum(pos + 1, size - 1)], 0)
    rim = (KWIN - QBLK) // 2
    lane_block = head_lanes(LANES)
    chunk = wsm_ref.shape[1]
    per = wsm_ref.shape[0] // HEADS
    wsm = wsm_ref[...]
    for kk in range(pair_ref.shape[1] // chunk):
        biased = mm(wsm, pair_ref[:, kk * chunk : (kk + 1) * chunk], NT)
        for g in range(blocks // GROUP):
            parts = [
                biased[h * per : (h + 1) * per, g * LANES : (g + 1) * LANES] for h in range(HEADS)
            ]
            for w, out in enumerate(lane_swap(parts, lane_block)):
                b = g * GROUP + w
                slot = (
                    lax.broadcasted_iota(jnp.int32, (per, LANES), 0) + kk * per + b * QBLK - rim
                )
                alive = (
                    ((slot < 0) & (slot + rows < left))
                    | ((slot >= 0) & (slot < own))
                    | ((slot >= rows) & (slot - rows < right))
                )
                bias_scr[b, kk * per : (kk + 1) * per, :] = jnp.where(alive, out * LOG2E, -1e30)


def pair_gradient(pair_ref, score_scr, rsum_ref, blocks):
    lane_block = head_lanes(LANES)
    per = rsum_ref.shape[0] // HEADS
    chunk = rsum_ref.shape[1]
    total = None
    for kk in range(pair_ref.shape[1] // chunk):
        columns = []
        for g in range(blocks // GROUP):
            parts = [score_scr[g * GROUP + w, kk * per : (kk + 1) * per, :] for w in range(GROUP)]
            columns.append(jnp.concatenate(lane_swap(parts, lane_block), axis=0))
        grads = jnp.concatenate(columns, axis=1).astype(BF16)
        part = mm(grads, pair_ref[:, kk * chunk : (kk + 1) * chunk])
        total = part if total is None else total + part
    rsum_ref[...] = total


def main_kernel(
    counts_ref,
    atoms_ref,
    low_ref,
    high_ref,
    gain_ref,
    wq_ref,
    wk_ref,
    wv_ref,
    wg_ref,
    wo_ref,
    wt_ref,
    wsm_ref,
    pair_ref,
    ids_ref,
    cot_ref,
    pooled_ref,
    gupd_ref,
    dq_ref,
    dkv_ref,
    edge_low_ref,
    edge_high_ref,
    dg_ref,
    gout_ref,
    gtok_ref,
    rsum_ref,
    bias_scr,
    score_scr,
    member_scr,
    member_t_scr,
    inv_scr,
    wqg_scr,
    wkv_scr,
    hid_scr,
    q_scr,
    gate_scr,
    kv_scr,
    p_scr,
    plow_scr,
    att_scr,
    gatt_scr,
    acc_scr,
):
    step = pl.program_id(0)
    rows, width = q_scr.shape
    blocks = rows // QBLK
    rim = (KWIN - QBLK) // 2
    tokens = inv_scr.shape[0]
    scaling = (width // HEADS) ** (-0.5)
    lane_head = head_lanes(width)
    masks = [(lane_head == h).astype(F32).astype(BF16) for h in range(HEADS)]

    @pl.when(step == 0)
    def _():
        pos = lax.axis_index("seq")
        build_bias(counts_ref, pair_ref, wsm_ref, bias_scr, blocks, rows)
        token = lax.broadcasted_iota(jnp.int32, (tokens, rows), 0)
        slot = lax.broadcasted_iota(jnp.int32, (tokens, rows), 1)
        hit = (ids_ref[...] - pos * tokens == token) & (slot < counts_ref[pos])
        member_t = jnp.where(hit, 1.0, 0.0).astype(F32)
        inv_scr[...] = 1.0 / jnp.sum(member_t, axis=1, keepdims=True)
        member_t_scr[...] = member_t.astype(BF16)
        member_scr[...] = member_t.T.astype(BF16)
        wqg_scr[:, :width] = wq_ref[...]
        wqg_scr[:, width:] = wg_ref[...]
        wkv_scr[:, :width] = wk_ref[...]
        wkv_scr[:, width:] = wv_ref[...]
        score_scr[...] = jnp.zeros_like(score_scr)
        gout_ref[...] = jnp.zeros_like(gout_ref)
        gtok_ref[...] = jnp.zeros_like(gtok_ref)

    gain = gain_ref[...]
    x = atoms_ref[0].astype(F32)
    hid_scr[:rim] = layer_norm(low_ref[0].astype(F32), gain)[2]
    hid_scr[rim : rim + rows] = layer_norm(x, gain)[2]
    hid_scr[rim + rows :] = layer_norm(high_ref[0].astype(F32), gain)[2]
    kv_scr[...] = mm(hid_scr[...], wkv_scr[...]).astype(BF16)
    qg = mm(hid_scr[rim : rim + rows], wqg_scr[...])
    q_scr[...] = qg[:, :width].astype(BF16)
    gate_scr[...] = sigmoid(qg[:, width:])

    def forward(g, carry):
        for w in range(GROUP):
            b = g * GROUP + w
            at = pl.multiple_of(b * QBLK, QBLK)
            q_exp = expand(q_scr[pl.ds(at, QBLK), :], masks)
            keys = kv_scr[pl.ds(at, KWIN), :width]
            values = kv_scr[pl.ds(at, KWIN), width:]
            scores = mm(keys, q_exp, NT)
            e = jnp.exp2(scores * (scaling * LOG2E) + bias_scr[b])
            p = e * (1.0 / jnp.sum(e, axis=0, keepdims=True))
            p_scr[b] = p
            p_low = p.astype(BF16)
            plow_scr[b] = p_low
            att_scr[pl.ds(at, QBLK), :] = collapse(mm(p_low, values, TN), lane_head)
        return carry

    lax.fori_loop(0, blocks // GROUP, forward, 0)

    gate = gate_scr[...]
    att = att_scr[...]
    gated = (gate * att).astype(BF16)
    updated = (x + mm(gated, wo_ref[...])).astype(BF16)
    chunk = 256
    half = rows // 2
    scaled_cot = (cot_ref[0].astype(F32) * inv_scr[...]).astype(BF16)
    gupd = [None, None]
    for c in range(wt_ref.shape[1] // chunk):
        cols = slice(c * chunk, (c + 1) * chunk)
        wt = wt_ref[:, cols]
        pooled = None
        gtok = None
        for r in range(2):
            span = slice(r * half, (r + 1) * half)
            pre = mm(updated[span], wt)
            sig = sigmoid(pre)
            act = pre * sig
            grad_act = mm(member_scr[span, :], scaled_cot[:, cols])
            grad_pre = (grad_act * (sig + act * (1.0 - sig))).astype(BF16)
            part = mm(member_t_scr[:, span], act.astype(BF16))
            pooled = part if pooled is None else pooled + part
            part = mm(updated[span], grad_pre, TN)
            gtok = part if gtok is None else gtok + part
            part = mm(grad_pre, wt, NT)
            gupd[r] = part if gupd[r] is None else gupd[r] + part
        pooled_ref[0, :, cols] = (pooled * inv_scr[...]).astype(BF16)
        gtok_ref[:, cols] += gtok
    grad_updated = jnp.concatenate(gupd, axis=0).astype(BF16)
    gupd_ref[0] = grad_updated
    gout_ref[...] += mm(gated, grad_updated, TN)
    grad_gate = mm(grad_updated, wo_ref[...], NT) * gate
    gatt_scr[...] = grad_gate.astype(BF16)
    dg_ref[0] = (grad_gate * att * (1.0 - gate)).astype(BF16)
    acc_scr[...] = jnp.zeros_like(acc_scr)

    def backward(g, carry):
        for w in range(GROUP):
            b = g * GROUP + w
            at = pl.multiple_of(b * QBLK, QBLK)
            q_exp = expand(q_scr[pl.ds(at, QBLK), :], masks)
            g_exp = expand(gatt_scr[pl.ds(at, QBLK), :], masks)
            keys = kv_scr[pl.ds(at, KWIN), :width]
            values = kv_scr[pl.ds(at, KWIN), width:]
            p = p_scr[b]
            t = p * mm(values, g_exp, NT)
            ds = t - p * jnp.sum(t, axis=0, keepdims=True)
            score_scr[b] += ds
            ds_low = ds.astype(BF16)
            dq_ref[0, pl.ds(at, QBLK), :] = (
                collapse(mm(ds_low, keys, TN), lane_head) * scaling
            ).astype(BF16)
            acc_scr[pl.ds(at, KWIN), :width] += mm(ds_low, q_exp) * scaling
            acc_scr[pl.ds(at, KWIN), width:] += mm(plow_scr[b], g_exp)
        return carry

    lax.fori_loop(0, blocks // GROUP, backward, 0)
    edge_low_ref[0] = acc_scr[:rim].astype(BF16)
    edge_high_ref[0] = acc_scr[rim + rows :].astype(BF16)
    dkv_ref[0] = acc_scr[rim : rim + rows].astype(BF16)

    @pl.when(step == pl.num_programs(0) - 1)
    def _():
        pair_gradient(pair_ref, score_scr, rsum_ref, blocks)


def tail_kernel(
    atoms_ref,
    gain_ref,
    wq_ref,
    wk_ref,
    wv_ref,
    wg_ref,
    gupd_ref,
    dq_ref,
    dkv_ref,
    low_ref,
    high_ref,
    dg_ref,
    gatoms_ref,
    ggain_ref,
    gw_ref,
    d_scr,
    w_scr,
):
    step = pl.program_id(0)
    rows, width = atoms_ref.shape[1:]
    rim = low_ref.shape[1]

    @pl.when(step == 0)
    def _():
        for n, ref in enumerate((wq_ref, wk_ref, wv_ref, wg_ref)):
            w_scr[:, n * width : (n + 1) * width] = ref[...]
        ggain_ref[...] = jnp.zeros_like(ggain_ref)
        gw_ref[...] = jnp.zeros_like(gw_ref)

    gain = gain_ref[...]
    normed, inv_std, hidden = layer_norm(atoms_ref[0].astype(F32), gain)
    d_scr[:, :width] = dq_ref[0]
    d_scr[:, width : 3 * width] = dkv_ref[0]
    d_scr[:, 3 * width :] = dg_ref[0]
    d_scr[:rim, width : 3 * width] = (
        dkv_ref[0, :rim].astype(F32) + low_ref[0].astype(F32)
    ).astype(BF16)
    d_scr[rows - rim :, width : 3 * width] = (
        dkv_ref[0, rows - rim :].astype(F32) + high_ref[0].astype(F32)
    ).astype(BF16)
    d = d_scr[...]
    gw_ref[...] += mm(hidden, d, TN)
    grad_hidden = mm(d, w_scr[...], NT)
    gn = grad_hidden * normed
    ggain_ref[...] += jnp.sum(gn, axis=0, keepdims=True)
    gx = grad_hidden * gain
    grad_ln = inv_std * (
        gx
        - jnp.mean(gx, axis=-1, keepdims=True)
        - normed * jnp.mean(gn * gain, axis=-1, keepdims=True)
    )
    gatoms_ref[0] = (gupd_ref[0].astype(F32) + grad_ln).astype(BF16)


def per_sample(*shape):
    return pl.BlockSpec((1,) + shape, lambda s: (s,) + (0,) * len(shape))


def whole(*shape):
    return pl.BlockSpec(shape, lambda s: (0,) * len(shape))


def shifted(block, axis, distance):
    devices = range(lax.axis_size(axis))
    route = [(i - distance, i) for i in devices if i - distance in devices]
    return lax.ppermute(block, axis, route)


def on_device(
    atoms,
    gain,
    w_query,
    w_key,
    w_value,
    w_gate,
    w_out,
    w_token,
    w_pair,
    pair_cond,
    counts,
    membership,
    pooled_cot,
):
    samples, rows, width = atoms.shape
    blocks = rows // QBLK
    rim = (KWIN - QBLK) // 2
    tokens, token_width = pooled_cot.shape[1:]
    channels = w_pair.shape[0]
    per = 2 * LANES // channels
    low = shifted(atoms[:, rows - rim :], "seq", 1)
    high = shifted(atoms[:, :rim], "seq", -1)
    wsm = (
        w_pair.T[:, None, None, :] * jnp.eye(per, dtype=BF16)[None, :, :, None]
    ).reshape(HEADS * per, per * channels)
    pair2 = pair_cond.reshape(blocks * QBLK, pair_cond.shape[-1])
    gain2 = gain.reshape(1, width)
    square = whole(width, width)
    params = pltpu.CompilerParams(
        dimension_semantics=("arbitrary",), vmem_limit_bytes=56 * 1024 * 1024
    )
    shape = jax.ShapeDtypeStruct
    (pooled, gupd, dq, dkv, edge_low, edge_high, dg, gout, gtok, rsum) = pl.pallas_call(
        main_kernel,
        grid=(samples,),
        in_specs=[
            pl.BlockSpec(memory_space=pltpu.SMEM),
            per_sample(rows, width),
            per_sample(rim, width),
            per_sample(rim, width),
            whole(1, width),
            square,
            square,
            square,
            square,
            square,
            whole(width, token_width),
            whole(*wsm.shape),
            whole(*pair2.shape),
            whole(1, rows),
            per_sample(tokens, token_width),
        ],
        out_specs=[
            per_sample(tokens, token_width),
            per_sample(rows, width),
            per_sample(rows, width),
            per_sample(rows, 2 * width),
            per_sample(rim, 2 * width),
            per_sample(rim, 2 * width),
            per_sample(rows, width),
            square,
            whole(width, token_width),
            whole(*wsm.shape),
        ],
        out_shape=[
            shape((samples, tokens, token_width), BF16),
            shape((samples, rows, width), BF16),
            shape((samples, rows, width), BF16),
            shape((samples, rows, 2 * width), BF16),
            shape((samples, rim, 2 * width), BF16),
            shape((samples, rim, 2 * width), BF16),
            shape((samples, rows, width), BF16),
            shape((width, width), F32),
            shape((width, token_width), F32),
            shape(wsm.shape, F32),
        ],
        scratch_shapes=[
            pltpu.VMEM((blocks, KWIN, LANES), F32),
            pltpu.VMEM((blocks, KWIN, LANES), F32),
            pltpu.VMEM((rows, tokens), BF16),
            pltpu.VMEM((tokens, rows), BF16),
            pltpu.VMEM((tokens, 1), F32),
            pltpu.VMEM((width, 2 * width), BF16),
            pltpu.VMEM((width, 2 * width), BF16),
            pltpu.VMEM((rows + 2 * rim, width), BF16),
            pltpu.VMEM((rows, width), BF16),
            pltpu.VMEM((rows, width), F32),
            pltpu.VMEM((rows + 2 * rim, 2 * width), BF16),
            pltpu.VMEM((blocks, KWIN, LANES), F32),
            pltpu.VMEM((blocks, KWIN, LANES), BF16),
            pltpu.VMEM((rows, width), F32),
            pltpu.VMEM((rows, width), BF16),
            pltpu.VMEM((rows + 2 * rim, 2 * width), F32),
        ],
        compiler_params=params,
    )(
        counts,
        atoms,
        low,
        high,
        gain2,
        w_query,
        w_key,
        w_value,
        w_gate,
        w_out,
        w_token,
        wsm,
        pair2,
        membership.reshape(1, rows),
        pooled_cot,
    )
    from_left = shifted(edge_high, "seq", 1)
    from_right = shifted(edge_low, "seq", -1)
    grad_atoms, ggain, gw = pl.pallas_call(
        tail_kernel,
        grid=(samples,),
        in_specs=[
            per_sample(rows, width),
            whole(1, width),
            square,
            square,
            square,
            square,
            per_sample(rows, width),
            per_sample(rows, width),
            per_sample(rows, 2 * width),
            per_sample(rim, 2 * width),
            per_sample(rim, 2 * width),
            per_sample(rows, width),
        ],
        out_specs=[per_sample(rows, width), whole(1, width), whole(width, 4 * width)],
        out_shape=[
            shape((samples, rows, width), BF16),
            shape((1, width), F32),
            shape((width, 4 * width), F32),
        ],
        scratch_shapes=[
            pltpu.VMEM((rows, 4 * width), BF16),
            pltpu.VMEM((width, 4 * width), BF16),
        ],
        compiler_params=params,
    )(
        atoms,
        gain2,
        w_query,
        w_key,
        w_value,
        w_gate,
        gupd,
        dq,
        dkv,
        from_left,
        from_right,
        dg,
    )
    gpair = jnp.einsum("hjjc->ch", rsum.reshape(HEADS, per, per, channels))
    gout, gtok, gpair, ggain, gw = lax.psum((gout, gtok, gpair, ggain, gw), ("seq", "samp"))
    gq, gk, gv, gg = (gw[:, n * width : (n + 1) * width] for n in range(4))
    return (pooled, grad_atoms, ggain.reshape(width), gq, gk, gv, gg, gout, gtok, gpair)


def solution(mesh):
    placed = (
        P("samp", "seq", None),
        P(),
        P(),
        P(),
        P(),
        P(),
        P(),
        P(),
        P(),
        P("seq", None, None),
        P(),
        P("seq"),
        P("samp", "seq", None),
    )
    return jax.shard_map(
        on_device,
        mesh=mesh,
        in_specs=placed,
        out_specs=(
            P("samp", "seq", None),
            P("samp", "seq", None),
            P(),
            P(),
            P(),
            P(),
            P(),
            P(),
            P(),
            P(),
        ),
        check_vma=False,
    )
```

```python
import functools

import jax
import jax.numpy as jnp
from jax import lax
from jax.experimental import pallas as pl
from jax.experimental.pallas import tpu as pltpu
from jax.sharding import PartitionSpec as P

HEADS = 4
QBLK = 32
KWIN = 128
LOG2E = 1.4426950408889634

epsilon = 1e-05
F32 = jnp.float32
BF16 = jnp.bfloat16
NN = (((1,), (0,)), ((), ()))
NT = (((1,), (1,)), ((), ()))
TN = (((0,), (0,)), ((), ()))
GROUP = 4
LANES = 128


def mm(a, b, dims=NN):
    return lax.dot_general(a, b, dims, preferred_element_type=F32)


def sigmoid(x):
    return 0.5 * jnp.tanh(0.5 * x) + 0.5


def layer_norm(x, gain):
    centred = x - jnp.mean(x, axis=-1, keepdims=True)
    variance = jnp.mean(centred * centred, axis=-1, keepdims=True)
    inv_std = lax.rsqrt(variance + epsilon)
    normed = centred * inv_std
    return normed, inv_std, (normed * gain).astype(BF16)


def head_lanes(width):
    lane = lax.broadcasted_iota(jnp.int32, (1, width), 1)
    return lane // (width // HEADS)


def expand(block, masks):
    return jnp.concatenate([block * m for m in masks], axis=0)


def collapse(wide, lane_head):
    rows = wide.shape[0] // HEADS
    out = wide[:rows]
    for h in range(1, HEADS):
        out = jnp.where(lane_head == h, wide[h * rows : (h + 1) * rows], out)
    return out


def lane_swap(parts, lane_block):
    count = len(parts)
    outs = []
    for b in range(count):
        out = None
        for a in range(count):
            shift = (QBLK * (a - b)) % LANES
            moved = parts[a] if shift == 0 else pltpu.roll(parts[a], shift, 1)
            out = moved if out is None else jnp.where(lane_block == a, moved, out)
        outs.append(out)
    return outs


def build_bias(counts_ref, pair_ref, wsm_ref, bias_scr, blocks, rows):
    pos = lax.axis_index("seq")
    size = lax.axis_size("seq")
    own = counts_ref[pos]
    left = jnp.where(pos > 0, counts_ref[jnp.maximum(pos - 1, 0)], 0)
    right = jnp.where(pos < size - 1, counts_ref[jnp.minimum(pos + 1, size - 1)], 0)
    rim = (KWIN - QBLK) // 2
    lane_block = head_lanes(LANES)
    chunk = wsm_ref.shape[1]
    per = wsm_ref.shape[0] // HEADS
    wsm = wsm_ref[...]
    for kk in range(pair_ref.shape[1] // chunk):
        biased = mm(wsm, pair_ref[:, kk * chunk : (kk + 1) * chunk], NT)
        for g in range(blocks // GROUP):
            parts = [
                biased[h * per : (h + 1) * per, g * LANES : (g + 1) * LANES] for h in range(HEADS)
            ]
            for w, out in enumerate(lane_swap(parts, lane_block)):
                b = g * GROUP + w
                slot = (
                    lax.broadcasted_iota(jnp.int32, (per, LANES), 0) + kk * per + b * QBLK - rim
                )
                alive = (
                    ((slot < 0) & (slot + rows < left))
                    | ((slot >= 0) & (slot < own))
                    | ((slot >= rows) & (slot - rows < right))
                )
                bias_scr[b, kk * per : (kk + 1) * per, :] = jnp.where(alive, out * LOG2E, -1e30)


def pair_gradient(pair_ref, score_scr, rsum_ref, blocks):
    lane_block = head_lanes(LANES)
    per = rsum_ref.shape[0] // HEADS
    chunk = rsum_ref.shape[1]
    total = None
    for kk in range(pair_ref.shape[1] // chunk):
        columns = []
        for g in range(blocks // GROUP):
            parts = [score_scr[g * GROUP + w, kk * per : (kk + 1) * per, :] for w in range(GROUP)]
            columns.append(jnp.concatenate(lane_swap(parts, lane_block), axis=0))
        grads = jnp.concatenate(columns, axis=1).astype(BF16)
        part = mm(grads, pair_ref[:, kk * chunk : (kk + 1) * chunk])
        total = part if total is None else total + part
    rsum_ref[...] = total


def main_kernel(
    counts_ref,
    atoms_ref,
    low_ref,
    high_ref,
    gain_ref,
    wq_ref,
    wk_ref,
    wv_ref,
    wg_ref,
    wo_ref,
    wt_ref,
    wsm_ref,
    pair_ref,
    ids_ref,
    cot_ref,
    pooled_ref,
    gupd_ref,
    dq_ref,
    dkv_ref,
    edge_low_ref,
    edge_high_ref,
    dg_ref,
    gout_ref,
    gtok_ref,
    rsum_ref,
    bias_scr,
    score_scr,
    member_scr,
    member_t_scr,
    inv_scr,
    wqg_scr,
    wkv_scr,
    hid_scr,
    q_scr,
    gate_scr,
    kv_scr,
    p_scr,
    plow_scr,
    att_scr,
    gatt_scr,
    acc_scr,
):
    step = pl.program_id(0)
    rows, width = q_scr.shape
    blocks = rows // QBLK
    rim = (KWIN - QBLK) // 2
    tokens = inv_scr.shape[0]
    scaling = (width // HEADS) ** (-0.5)
    lane_head = head_lanes(width)
    masks = [(lane_head == h).astype(F32).astype(BF16) for h in range(HEADS)]

    @pl.when(step == 0)
    def _():
        pos = lax.axis_index("seq")
        build_bias(counts_ref, pair_ref, wsm_ref, bias_scr, blocks, rows)
        token = lax.broadcasted_iota(jnp.int32, (tokens, rows), 0)
        slot = lax.broadcasted_iota(jnp.int32, (tokens, rows), 1)
        hit = (ids_ref[...] - pos * tokens == token) & (slot < counts_ref[pos])
        member_t = jnp.where(hit, 1.0, 0.0).astype(F32)
        inv_scr[...] = 1.0 / jnp.sum(member_t, axis=1, keepdims=True)
        member_t_scr[...] = member_t.astype(BF16)
        member_scr[...] = member_t.T.astype(BF16)
        wqg_scr[:, :width] = wq_ref[...]
        wqg_scr[:, width:] = wg_ref[...]
        wkv_scr[:, :width] = wk_ref[...]
        wkv_scr[:, width:] = wv_ref[...]
        score_scr[...] = jnp.zeros_like(score_scr)
        gout_ref[...] = jnp.zeros_like(gout_ref)
        gtok_ref[...] = jnp.zeros_like(gtok_ref)

    gain = gain_ref[...]
    x = atoms_ref[0].astype(F32)
    hid_scr[:rim] = layer_norm(low_ref[0].astype(F32), gain)[2]
    hid_scr[rim : rim + rows] = layer_norm(x, gain)[2]
    hid_scr[rim + rows :] = layer_norm(high_ref[0].astype(F32), gain)[2]
    kv_scr[...] = mm(hid_scr[...], wkv_scr[...]).astype(BF16)
    qg = mm(hid_scr[rim : rim + rows], wqg_scr[...])
    q_scr[...] = qg[:, :width].astype(BF16)
    gate_scr[...] = sigmoid(qg[:, width:])

    for g in range(blocks // GROUP):
        spans = [g * GROUP + w for w in range(GROUP)]
        q_exp = [expand(q_scr[b * QBLK : (b + 1) * QBLK, :], masks) for b in spans]
        scores = [
            mm(kv_scr[b * QBLK : b * QBLK + KWIN, :width], q, NT) for b, q in zip(spans, q_exp)
        ]
        es = [
            jnp.exp2(sc * (scaling * LOG2E) + bias_scr[b]) for b, sc in zip(spans, scores)
        ]
        invs = [1.0 / jnp.sum(e, axis=0, keepdims=True) for e in es]
        ps = [e * inv for e, inv in zip(es, invs)]
        lows = [p.astype(BF16) for p in ps]
        for b, p, low in zip(spans, ps, lows):
            p_scr[b] = p
            plow_scr[b] = low
        wide = [
            mm(low, kv_scr[b * QBLK : b * QBLK + KWIN, width:], TN)
            for b, low in zip(spans, lows)
        ]
        for b, o in zip(spans, wide):
            att_scr[b * QBLK : (b + 1) * QBLK, :] = collapse(o, lane_head)

    gate = gate_scr[...]
    att = att_scr[...]
    gated = (gate * att).astype(BF16)
    updated = (x + mm(gated, wo_ref[...])).astype(BF16)
    chunk = 256
    half = rows // 2
    scaled_cot = (cot_ref[0].astype(F32) * inv_scr[...]).astype(BF16)
    gupd = [None, None]
    for c in range(wt_ref.shape[1] // chunk):
        cols = slice(c * chunk, (c + 1) * chunk)
        wt = wt_ref[:, cols]
        pooled = None
        gtok = None
        for r in range(2):
            span = slice(r * half, (r + 1) * half)
            pre = mm(updated[span], wt)
            sig = sigmoid(pre)
            act = pre * sig
            grad_act = mm(member_scr[span, :], scaled_cot[:, cols])
            grad_pre = (grad_act * (sig + act * (1.0 - sig))).astype(BF16)
            part = mm(member_t_scr[:, span], act.astype(BF16))
            pooled = part if pooled is None else pooled + part
            part = mm(updated[span], grad_pre, TN)
            gtok = part if gtok is None else gtok + part
            part = mm(grad_pre, wt, NT)
            gupd[r] = part if gupd[r] is None else gupd[r] + part
        pooled_ref[0, :, cols] = (pooled * inv_scr[...]).astype(BF16)
        gtok_ref[:, cols] += gtok
    grad_updated = jnp.concatenate(gupd, axis=0).astype(BF16)
    gupd_ref[0] = grad_updated
    gout_ref[...] += mm(gated, grad_updated, TN)
    grad_gate = mm(grad_updated, wo_ref[...], NT) * gate
    gatt_scr[...] = grad_gate.astype(BF16)
    dg_ref[0] = (grad_gate * att * (1.0 - gate)).astype(BF16)

    def tiles(x):
        return [x[n * QBLK : (n + 1) * QBLK] for n in range(KWIN // QBLK)]

    open_k = []
    open_v = []

    def close(first, count):
        for n in range(count):
            at = (first + n) * QBLK
            acc_scr[at : at + QBLK, :width] = open_k[n] * scaling
            acc_scr[at : at + QBLK, width:] = open_v[n]
        del open_k[:count]
        del open_v[:count]

    def merge(opened, parts):
        for n, part in enumerate(parts):
            if n < len(opened):
                opened[n] = opened[n] + part
            else:
                opened.append(part)

    for g in range(blocks // GROUP):
        spans = [g * GROUP + w for w in range(GROUP)]
        g_exp = [expand(gatt_scr[b * QBLK : (b + 1) * QBLK, :], masks) for b in spans]
        gps = [
            mm(kv_scr[b * QBLK : b * QBLK + KWIN, width:], ge, NT) for b, ge in zip(spans, g_exp)
        ]
        dvs = [mm(plow_scr[b], ge) for b, ge in zip(spans, g_exp)]
        ts = [p_scr[b] * gp for b, gp in zip(spans, gps)]
        sums = [jnp.sum(t, axis=0, keepdims=True) for t in ts]
        dss = [t - p_scr[b] * r for b, t, r in zip(spans, ts, sums)]
        lows = [ds.astype(BF16) for ds in dss]
        for b, ds in zip(spans, dss):
            score_scr[b] += ds
        q_exp = [expand(q_scr[b * QBLK : (b + 1) * QBLK, :], masks) for b in spans]
        dks = [mm(low, q) for low, q in zip(lows, q_exp)]
        dqs = [
            mm(low, kv_scr[b * QBLK : b * QBLK + KWIN, :width], TN)
            for b, low in zip(spans, lows)
        ]
        for b, dk, dv in zip(spans, dks, dvs):
            merge(open_k, tiles(dk))
            merge(open_v, tiles(dv))
            close(b, 1)
        for b, dq in zip(spans, dqs):
            dq_ref[0, b * QBLK : (b + 1) * QBLK, :] = (
                collapse(dq, lane_head) * scaling
            ).astype(BF16)
    close(blocks, len(open_k))
    edge_low_ref[0] = acc_scr[:rim].astype(BF16)
    edge_high_ref[0] = acc_scr[rim + rows :].astype(BF16)
    dkv_ref[0] = acc_scr[rim : rim + rows].astype(BF16)

    @pl.when(step == pl.num_programs(0) - 1)
    def _():
        pair_gradient(pair_ref, score_scr, rsum_ref, blocks)


def tail_kernel(
    atoms_ref,
    gain_ref,
    wq_ref,
    wk_ref,
    wv_ref,
    wg_ref,
    gupd_ref,
    dq_ref,
    dkv_ref,
    low_ref,
    high_ref,
    dg_ref,
    gatoms_ref,
    ggain_ref,
    gw_ref,
    d_scr,
    w_scr,
):
    step = pl.program_id(0)
    rows, width = atoms_ref.shape[1:]
    rim = low_ref.shape[1]

    @pl.when(step == 0)
    def _():
        for n, ref in enumerate((wq_ref, wk_ref, wv_ref, wg_ref)):
            w_scr[:, n * width : (n + 1) * width] = ref[...]
        ggain_ref[...] = jnp.zeros_like(ggain_ref)
        gw_ref[...] = jnp.zeros_like(gw_ref)

    gain = gain_ref[...]
    normed, inv_std, hidden = layer_norm(atoms_ref[0].astype(F32), gain)
    d_scr[:, :width] = dq_ref[0]
    d_scr[:, width : 3 * width] = dkv_ref[0]
    d_scr[:, 3 * width :] = dg_ref[0]
    d_scr[:rim, width : 3 * width] = (
        dkv_ref[0, :rim].astype(F32) + low_ref[0].astype(F32)
    ).astype(BF16)
    d_scr[rows - rim :, width : 3 * width] = (
        dkv_ref[0, rows - rim :].astype(F32) + high_ref[0].astype(F32)
    ).astype(BF16)
    d = d_scr[...]
    gw_ref[...] += mm(hidden, d, TN)
    grad_hidden = mm(d, w_scr[...], NT)
    gn = grad_hidden * normed
    ggain_ref[...] += jnp.sum(gn, axis=0, keepdims=True)
    gx = grad_hidden * gain
    grad_ln = inv_std * (
        gx
        - jnp.mean(gx, axis=-1, keepdims=True)
        - normed * jnp.mean(gn * gain, axis=-1, keepdims=True)
    )
    gatoms_ref[0] = (gupd_ref[0].astype(F32) + grad_ln).astype(BF16)


def axis_bits():
    bits = []
    for axis in ("samp", "seq"):
        bit = 1
        while bit < lax.axis_size(axis):
            bits.append((axis, bit))
            bit *= 2
    return bits


def sum_kernel(
    gout_ref,
    gtok_ref,
    gw_ref,
    rsum_ref,
    ggain_ref,
    gq_out,
    gk_out,
    gv_out,
    gg_out,
    gout_out,
    gtok_out,
    small_out,
    buf,
    gbuf,
    send_sem,
    recv_sem,
    *slots,
):
    bits = axis_bits()
    count = len(bits)
    sends, recvs = slots[:count], slots[count:]
    width = gout_ref.shape[0]
    where = []
    for axis, bit in bits:
        me = lax.axis_index(axis)
        upper = lax.rem(me // bit, 2)
        where.append((upper, {axis: me + bit - 2 * bit * upper}))
    barrier = pltpu.get_barrier_semaphore()
    for _, partner in where:
        pl.semaphore_signal(
            barrier, inc=1, device_id=partner, device_id_type=pl.DeviceIdType.MESH
        )

    blocks = gtok_ref.shape[1] // width
    for n in range(blocks):
        buf[n * width : (n + 1) * width, :] = gtok_ref[:, n * width : (n + 1) * width]
    for n in range(4):
        at = (blocks + n) * width
        buf[at : at + width, :] = gw_ref[:, n * width : (n + 1) * width]
    at = (blocks + 4) * width
    buf[at : at + width, :] = gout_ref[...]
    at += width
    buf[at:, :] = jnp.zeros((buf.shape[0] - at, width), F32)
    high, wide = rsum_ref.shape
    per = high // HEADS
    row = lax.broadcasted_iota(jnp.int32, (high, wide), 0)
    lane = lax.broadcasted_iota(jnp.int32, (high, wide), 1)
    diagonal = jnp.where(lax.rem(row, per) == lane // (wide // per), rsum_ref[...], 0.0)
    for h in range(HEADS):
        line = jnp.sum(diagonal[h * per : (h + 1) * per], axis=0, keepdims=True)
        for n in range(wide // width):
            buf[at + n * HEADS + h : at + n * HEADS + h + 1, :] = line[
                :, n * width : (n + 1) * width
            ]
    spot = at + HEADS * (wide // width)
    buf[spot : spot + 1, :] = ggain_ref[...]
    pl.semaphore_wait(barrier, count)

    off = 0
    length = buf.shape[0]
    for k, (upper, partner) in enumerate(where):
        length //= 2
        keep = pl.multiple_of(off + upper * length, 16)
        give = pl.multiple_of(off + (1 - upper) * length, 16)
        sends[k][...] = buf[pl.ds(give, length), :].astype(BF16)
        copy = pltpu.make_async_remote_copy(
            src_ref=sends[k],
            dst_ref=recvs[k],
            send_sem=send_sem.at[k],
            recv_sem=recv_sem.at[k],
            device_id=partner,
            device_id_type=pl.DeviceIdType.MESH,
        )
        copy.start()
        copy.wait()
        buf[pl.ds(keep, length), :] = buf[pl.ds(keep, length), :] + recvs[k][...].astype(F32)
        off = keep
    gbuf[pl.ds(off, length), :] = buf[pl.ds(off, length), :].astype(BF16)
    for k in range(count - 1, -1, -1):
        upper, partner = where[k]
        part = gbuf.at[pl.ds(pl.multiple_of(off, 16), length), :]
        copy = pltpu.make_async_remote_copy(
            src_ref=part,
            dst_ref=part,
            send_sem=send_sem.at[count + k],
            recv_sem=recv_sem.at[count + k],
            device_id=partner,
            device_id_type=pl.DeviceIdType.MESH,
        )
        copy.start()
        copy.wait()
        off = off - upper * length
        length *= 2

    def block(n):
        return gbuf[n * width : (n + 1) * width, :].astype(F32)

    for n in range(blocks):
        gtok_out[:, n * width : (n + 1) * width] = block(n)
    for n, ref in enumerate((gq_out, gk_out, gv_out, gg_out, gout_out)):
        ref[...] = block(blocks + n)
    small_out[...] = gbuf[at : at + small_out.shape[0], :].astype(F32)


def sum_all(gout, gtok, gw, rsum, ggain):
    shape = jax.ShapeDtypeStruct
    width = gout.shape[0]
    bits = axis_bits()
    count = len(bits)
    unit = 16 * 2**count
    lines = gtok.shape[1] + gw.shape[1] + width + 16
    total = -(-lines // unit) * unit
    slots = [pltpu.VMEM((total >> (k + 1), width), BF16) for k in range(count)]
    return pl.pallas_call(
        sum_kernel,
        in_specs=[pl.BlockSpec(memory_space=pltpu.VMEM)] * 5,
        out_specs=[pl.BlockSpec(memory_space=pltpu.VMEM)] * 7,
        out_shape=[shape((width, width), F32)] * 5
        + [shape(gtok.shape, F32), shape((16, width), F32)],
        scratch_shapes=[
            pltpu.VMEM((total, width), F32),
            pltpu.VMEM((total, width), BF16),
            pltpu.SemaphoreType.DMA((2 * count,)),
            pltpu.SemaphoreType.DMA((2 * count,)),
        ]
        + slots
        + slots,
        compiler_params=pltpu.CompilerParams(collective_id=0, has_side_effects=True),
    )(gout, gtok, gw, rsum, ggain)


def per_sample(*shape):
    return pl.BlockSpec((1,) + shape, lambda s: (s,) + (0,) * len(shape))


def whole(*shape):
    return pl.BlockSpec(shape, lambda s: (0,) * len(shape))


def shifted(block, axis, distance):
    devices = range(lax.axis_size(axis))
    route = [(i - distance, i) for i in devices if i - distance in devices]
    return lax.ppermute(block, axis, route)


def on_device(
    atoms,
    gain,
    w_query,
    w_key,
    w_value,
    w_gate,
    w_out,
    w_token,
    w_pair,
    pair_cond,
    counts,
    membership,
    pooled_cot,
):
    samples, rows, width = atoms.shape
    blocks = rows // QBLK
    rim = (KWIN - QBLK) // 2
    tokens, token_width = pooled_cot.shape[1:]
    channels = w_pair.shape[0]
    per = 2 * LANES // channels
    low = shifted(atoms[:, rows - rim :], "seq", 1)
    high = shifted(atoms[:, :rim], "seq", -1)
    wsm = (
        w_pair.T[:, None, None, :] * jnp.eye(per, dtype=BF16)[None, :, :, None]
    ).reshape(HEADS * per, per * channels)
    pair2 = pair_cond.reshape(blocks * QBLK, pair_cond.shape[-1])
    gain2 = gain.reshape(1, width)
    square = whole(width, width)
    params = pltpu.CompilerParams(
        dimension_semantics=("arbitrary",), vmem_limit_bytes=56 * 1024 * 1024
    )
    shape = jax.ShapeDtypeStruct
    (pooled, gupd, dq, dkv, edge_low, edge_high, dg, gout, gtok, rsum) = pl.pallas_call(
        main_kernel,
        grid=(samples,),
        in_specs=[
            pl.BlockSpec(memory_space=pltpu.SMEM),
            per_sample(rows, width),
            per_sample(rim, width),
            per_sample(rim, width),
            whole(1, width),
            square,
            square,
            square,
            square,
            square,
            whole(width, token_width),
            whole(*wsm.shape),
            whole(*pair2.shape),
            whole(1, rows),
            per_sample(tokens, token_width),
        ],
        out_specs=[
            per_sample(tokens, token_width),
            per_sample(rows, width),
            per_sample(rows, width),
            per_sample(rows, 2 * width),
            per_sample(rim, 2 * width),
            per_sample(rim, 2 * width),
            per_sample(rows, width),
            square,
            whole(width, token_width),
            whole(*wsm.shape),
        ],
        out_shape=[
            shape((samples, tokens, token_width), BF16),
            shape((samples, rows, width), BF16),
            shape((samples, rows, width), BF16),
            shape((samples, rows, 2 * width), BF16),
            shape((samples, rim, 2 * width), BF16),
            shape((samples, rim, 2 * width), BF16),
            shape((samples, rows, width), BF16),
            shape((width, width), F32),
            shape((width, token_width), F32),
            shape(wsm.shape, F32),
        ],
        scratch_shapes=[
            pltpu.VMEM((blocks, KWIN, LANES), F32),
            pltpu.VMEM((blocks, KWIN, LANES), F32),
            pltpu.VMEM((rows, tokens), BF16),
            pltpu.VMEM((tokens, rows), BF16),
            pltpu.VMEM((tokens, 1), F32),
            pltpu.VMEM((width, 2 * width), BF16),
            pltpu.VMEM((width, 2 * width), BF16),
            pltpu.VMEM((rows + 2 * rim, width), BF16),
            pltpu.VMEM((rows, width), BF16),
            pltpu.VMEM((rows, width), F32),
            pltpu.VMEM((rows + 2 * rim, 2 * width), BF16),
            pltpu.VMEM((blocks, KWIN, LANES), F32),
            pltpu.VMEM((blocks, KWIN, LANES), BF16),
            pltpu.VMEM((rows, width), F32),
            pltpu.VMEM((rows, width), BF16),
            pltpu.VMEM((rows + 2 * rim, 2 * width), F32),
        ],
        compiler_params=params,
    )(
        counts,
        atoms,
        low,
        high,
        gain2,
        w_query,
        w_key,
        w_value,
        w_gate,
        w_out,
        w_token,
        wsm,
        pair2,
        membership.reshape(1, rows),
        pooled_cot,
    )
    from_left = shifted(edge_high, "seq", 1)
    from_right = shifted(edge_low, "seq", -1)
    grad_atoms, ggain, gw = pl.pallas_call(
        tail_kernel,
        grid=(samples,),
        in_specs=[
            per_sample(rows, width),
            whole(1, width),
            square,
            square,
            square,
            square,
            per_sample(rows, width),
            per_sample(rows, width),
            per_sample(rows, 2 * width),
            per_sample(rim, 2 * width),
            per_sample(rim, 2 * width),
            per_sample(rows, width),
        ],
        out_specs=[per_sample(rows, width), whole(1, width), whole(width, 4 * width)],
        out_shape=[
            shape((samples, rows, width), BF16),
            shape((1, width), F32),
            shape((width, 4 * width), F32),
        ],
        scratch_shapes=[
            pltpu.VMEM((rows, 4 * width), BF16),
            pltpu.VMEM((width, 4 * width), BF16),
        ],
        compiler_params=params,
    )(
        atoms,
        gain2,
        w_query,
        w_key,
        w_value,
        w_gate,
        gupd,
        dq,
        dkv,
        from_left,
        from_right,
        dg,
    )
    gq, gk, gv, gg, gout, gtok, small = sum_all(gout, gtok, gw, rsum, ggain)
    halves = rsum.shape[1] // width
    lines = small[: halves * HEADS].reshape(halves, HEADS, width // channels, channels)
    gpair = jnp.sum(lines, axis=(0, 2)).T
    ggain = small[halves * HEADS]
    return (pooled, grad_atoms, ggain, gq, gk, gv, gg, gout, gtok, gpair)


def solution(mesh):
    placed = (
        P("samp", "seq", None),
        P(),
        P(),
        P(),
        P(),
        P(),
        P(),
        P(),
        P(),
        P("seq", None, None),
        P(),
        P("seq"),
        P("samp", "seq", None),
    )
    return jax.shard_map(
        on_device,
        mesh=mesh,
        in_specs=placed,
        out_specs=(
            P("samp", "seq", None),
            P("samp", "seq", None),
            P(),
            P(),
            P(),
            P(),
            P(),
            P(),
            P(),
            P(),
        ),
        check_vma=False,
    )
```

```python
import functools

import jax
import jax.numpy as jnp
from jax import lax
from jax.experimental import pallas as pl
from jax.experimental.pallas import tpu as pltpu
from jax.sharding import PartitionSpec as P

HEADS = 4
QBLK = 32
KWIN = 128
LOG2E = 1.4426950408889634

epsilon = 1e-05
F32 = jnp.float32
BF16 = jnp.bfloat16
NN = (((1,), (0,)), ((), ()))
NT = (((1,), (1,)), ((), ()))
TN = (((0,), (0,)), ((), ()))
GROUP = 4
LANES = 128


def mm(a, b, dims=NN):
    return lax.dot_general(a, b, dims, preferred_element_type=F32)


def sigmoid(x):
    return 0.5 * jnp.tanh(0.5 * x) + 0.5


def layer_norm(x, gain):
    centred = x - jnp.mean(x, axis=-1, keepdims=True)
    variance = jnp.mean(centred * centred, axis=-1, keepdims=True)
    inv_std = lax.rsqrt(variance + epsilon)
    normed = centred * inv_std
    return normed, inv_std, (normed * gain).astype(BF16)


def head_lanes(width):
    lane = lax.broadcasted_iota(jnp.int32, (1, width), 1)
    return lane // (width // HEADS)


def expand(block, masks):
    return jnp.concatenate([block * m for m in masks], axis=0)


def collapse(wide, lane_head):
    rows = wide.shape[0] // HEADS
    out = wide[:rows]
    for h in range(1, HEADS):
        out = jnp.where(lane_head == h, wide[h * rows : (h + 1) * rows], out)
    return out


def lane_swap(parts, lane_block):
    count = len(parts)
    outs = []
    for b in range(count):
        out = None
        for a in range(count):
            shift = (QBLK * (a - b)) % LANES
            moved = parts[a] if shift == 0 else pltpu.roll(parts[a], shift, 1)
            out = moved if out is None else jnp.where(lane_block == a, moved, out)
        outs.append(out)
    return outs


def build_bias(counts_ref, pair_ref, wsm_ref, bias_scr, blocks, rows):
    pos = lax.axis_index("seq")
    size = lax.axis_size("seq")
    own = counts_ref[pos]
    left = jnp.where(pos > 0, counts_ref[jnp.maximum(pos - 1, 0)], 0)
    right = jnp.where(pos < size - 1, counts_ref[jnp.minimum(pos + 1, size - 1)], 0)
    rim = (KWIN - QBLK) // 2
    lane_block = head_lanes(LANES)
    chunk = wsm_ref.shape[1]
    per = wsm_ref.shape[0] // HEADS
    wsm = wsm_ref[...]
    for kk in range(pair_ref.shape[1] // chunk):
        biased = mm(wsm, pair_ref[:, kk * chunk : (kk + 1) * chunk], NT)
        for g in range(blocks // GROUP):
            parts = [
                biased[h * per : (h + 1) * per, g * LANES : (g + 1) * LANES] for h in range(HEADS)
            ]
            for w, out in enumerate(lane_swap(parts, lane_block)):
                b = g * GROUP + w
                slot = (
                    lax.broadcasted_iota(jnp.int32, (per, LANES), 0) + kk * per + b * QBLK - rim
                )
                alive = (
                    ((slot < 0) & (slot + rows < left))
                    | ((slot >= 0) & (slot < own))
                    | ((slot >= rows) & (slot - rows < right))
                )
                bias_scr[b, kk * per : (kk + 1) * per, :] = jnp.where(alive, out * LOG2E, -1e30)


def pair_gradient(pair_ref, score_scr, rsum_ref, blocks):
    lane_block = head_lanes(LANES)
    per = rsum_ref.shape[0] // HEADS
    chunk = rsum_ref.shape[1]
    total = None
    for kk in range(pair_ref.shape[1] // chunk):
        columns = []
        for g in range(blocks // GROUP):
            parts = [score_scr[g * GROUP + w, kk * per : (kk + 1) * per, :] for w in range(GROUP)]
            columns.append(jnp.concatenate(lane_swap(parts, lane_block), axis=0))
        grads = jnp.concatenate(columns, axis=1).astype(BF16)
        part = mm(grads, pair_ref[:, kk * chunk : (kk + 1) * chunk])
        total = part if total is None else total + part
    rsum_ref[...] = total


def main_kernel(
    counts_ref,
    atoms_ref,
    low_ref,
    high_ref,
    gain_ref,
    wq_ref,
    wk_ref,
    wv_ref,
    wg_ref,
    wo_ref,
    wt_ref,
    wsm_ref,
    pair_ref,
    ids_ref,
    cot_ref,
    pooled_ref,
    gupd_ref,
    dq_ref,
    dkv_ref,
    edge_low_ref,
    edge_high_ref,
    dg_ref,
    gout_ref,
    gtok_ref,
    rsum_ref,
    bias_scr,
    score_scr,
    member_scr,
    member_t_scr,
    inv_scr,
    wqg_scr,
    wkv_scr,
    hid_scr,
    q_scr,
    gate_scr,
    kv_scr,
    p_scr,
    plow_scr,
    att_scr,
    gatt_scr,
    acc_scr,
):
    step = pl.program_id(0)
    rows, width = q_scr.shape
    blocks = rows // QBLK
    rim = (KWIN - QBLK) // 2
    tokens = inv_scr.shape[0]
    scaling = (width // HEADS) ** (-0.5)
    lane_head = head_lanes(width)
    masks = [(lane_head == h).astype(F32).astype(BF16) for h in range(HEADS)]

    @pl.when(step == 0)
    def _():
        pos = lax.axis_index("seq")
        build_bias(counts_ref, pair_ref, wsm_ref, bias_scr, blocks, rows)
        token = lax.broadcasted_iota(jnp.int32, (tokens, rows), 0)
        slot = lax.broadcasted_iota(jnp.int32, (tokens, rows), 1)
        hit = (ids_ref[...] - pos * tokens == token) & (slot < counts_ref[pos])
        member_t = jnp.where(hit, 1.0, 0.0).astype(F32)
        inv_scr[...] = 1.0 / jnp.sum(member_t, axis=1, keepdims=True)
        member_t_scr[...] = member_t.astype(BF16)
        member_scr[...] = member_t.T.astype(BF16)
        wqg_scr[:, :width] = wq_ref[...]
        wqg_scr[:, width:] = wg_ref[...]
        wkv_scr[:, :width] = wk_ref[...]
        wkv_scr[:, width:] = wv_ref[...]
        score_scr[...] = jnp.zeros_like(score_scr)
        gout_ref[...] = jnp.zeros_like(gout_ref)
        gtok_ref[...] = jnp.zeros_like(gtok_ref)

    gain = gain_ref[...]
    x = atoms_ref[0].astype(F32)
    hid_scr[:rim] = layer_norm(low_ref[0].astype(F32), gain)[2]
    hid_scr[rim : rim + rows] = layer_norm(x, gain)[2]
    hid_scr[rim + rows :] = layer_norm(high_ref[0].astype(F32), gain)[2]
    kv_scr[...] = mm(hid_scr[...], wkv_scr[...]).astype(BF16)
    qg = mm(hid_scr[rim : rim + rows], wqg_scr[...])
    q_scr[...] = qg[:, :width].astype(BF16)
    gate_scr[...] = sigmoid(qg[:, width:])

    for g in range(blocks // GROUP):
        spans = [g * GROUP + w for w in range(GROUP)]
        q_exp = [expand(q_scr[b * QBLK : (b + 1) * QBLK, :], masks) for b in spans]
        scores = [
            mm(kv_scr[b * QBLK : b * QBLK + KWIN, :width], q, NT) for b, q in zip(spans, q_exp)
        ]
        es = [
            jnp.exp2(sc * (scaling * LOG2E) + bias_scr[b]) for b, sc in zip(spans, scores)
        ]
        invs = [1.0 / jnp.sum(e, axis=0, keepdims=True) for e in es]
        ps = [e * inv for e, inv in zip(es, invs)]
        lows = [p.astype(BF16) for p in ps]
        for b, p, low in zip(spans, ps, lows):
            p_scr[b] = p
            plow_scr[b] = low
        wide = [
            mm(low, kv_scr[b * QBLK : b * QBLK + KWIN, width:], TN)
            for b, low in zip(spans, lows)
        ]
        for b, o in zip(spans, wide):
            att_scr[b * QBLK : (b + 1) * QBLK, :] = collapse(o, lane_head)

    gate = gate_scr[...]
    att = att_scr[...]
    gated = (gate * att).astype(BF16)
    updated = (x + mm(gated, wo_ref[...])).astype(BF16)
    chunk = 256
    half = rows // 2
    scaled_cot = (cot_ref[0].astype(F32) * inv_scr[...]).astype(BF16)
    gupd = [None, None]
    for c in range(wt_ref.shape[1] // chunk):
        cols = slice(c * chunk, (c + 1) * chunk)
        wt = wt_ref[:, cols]
        pooled = None
        gtok = None
        for r in range(2):
            span = slice(r * half, (r + 1) * half)
            pre = mm(updated[span], wt)
            sig = sigmoid(pre)
            act = pre * sig
            grad_act = mm(member_scr[span, :], scaled_cot[:, cols])
            grad_pre = (grad_act * (sig + act * (1.0 - sig))).astype(BF16)
            part = mm(member_t_scr[:, span], act.astype(BF16))
            pooled = part if pooled is None else pooled + part
            part = mm(updated[span], grad_pre, TN)
            gtok = part if gtok is None else gtok + part
            part = mm(grad_pre, wt, NT)
            gupd[r] = part if gupd[r] is None else gupd[r] + part
        pooled_ref[0, :, cols] = (pooled * inv_scr[...]).astype(BF16)
        gtok_ref[:, cols] += gtok
    grad_updated = jnp.concatenate(gupd, axis=0).astype(BF16)
    gupd_ref[0] = grad_updated
    gout_ref[...] += mm(gated, grad_updated, TN)
    grad_gate = mm(grad_updated, wo_ref[...], NT) * gate
    gatt_scr[...] = grad_gate.astype(BF16)
    dg_ref[0] = (grad_gate * att * (1.0 - gate)).astype(BF16)

    def tiles(x):
        return [x[n * QBLK : (n + 1) * QBLK] for n in range(KWIN // QBLK)]

    open_k = []
    open_v = []

    def close(first, count):
        for n in range(count):
            at = (first + n) * QBLK
            acc_scr[at : at + QBLK, :width] = open_k[n] * scaling
            acc_scr[at : at + QBLK, width:] = open_v[n]
        del open_k[:count]
        del open_v[:count]

    def merge(opened, parts):
        for n, part in enumerate(parts):
            if n < len(opened):
                opened[n] = opened[n] + part
            else:
                opened.append(part)

    for g in range(blocks // GROUP):
        spans = [g * GROUP + w for w in range(GROUP)]
        g_exp = [expand(gatt_scr[b * QBLK : (b + 1) * QBLK, :], masks) for b in spans]
        gps = [
            mm(kv_scr[b * QBLK : b * QBLK + KWIN, width:], ge, NT) for b, ge in zip(spans, g_exp)
        ]
        dvs = [mm(plow_scr[b], ge) for b, ge in zip(spans, g_exp)]
        ts = [p_scr[b] * gp for b, gp in zip(spans, gps)]
        sums = [jnp.sum(t, axis=0, keepdims=True) for t in ts]
        dss = [t - p_scr[b] * r for b, t, r in zip(spans, ts, sums)]
        lows = [ds.astype(BF16) for ds in dss]
        for b, ds in zip(spans, dss):
            score_scr[b] += ds
        q_exp = [expand(q_scr[b * QBLK : (b + 1) * QBLK, :], masks) for b in spans]
        dks = [mm(low, q) for low, q in zip(lows, q_exp)]
        dqs = [
            mm(low, kv_scr[b * QBLK : b * QBLK + KWIN, :width], TN)
            for b, low in zip(spans, lows)
        ]
        for b, dk, dv in zip(spans, dks, dvs):
            merge(open_k, tiles(dk))
            merge(open_v, tiles(dv))
            close(b, 1)
        for b, dq in zip(spans, dqs):
            dq_ref[0, b * QBLK : (b + 1) * QBLK, :] = (
                collapse(dq, lane_head) * scaling
            ).astype(BF16)
    close(blocks, len(open_k))
    edge_low_ref[0] = acc_scr[:rim].astype(BF16)
    edge_high_ref[0] = acc_scr[rim + rows :].astype(BF16)
    dkv_ref[0] = acc_scr[rim : rim + rows].astype(BF16)

    @pl.when(step == pl.num_programs(0) - 1)
    def _():
        pair_gradient(pair_ref, score_scr, rsum_ref, blocks)


def tail_kernel(
    atoms_ref,
    gain_ref,
    wq_ref,
    wk_ref,
    wv_ref,
    wg_ref,
    gupd_ref,
    dq_ref,
    dkv_ref,
    low_ref,
    high_ref,
    dg_ref,
    gatoms_ref,
    ggain_ref,
    gw_ref,
    d_scr,
    w_scr,
):
    step = pl.program_id(0)
    rows, width = atoms_ref.shape[1:]
    rim = low_ref.shape[1]

    @pl.when(step == 0)
    def _():
        for n, ref in enumerate((wq_ref, wk_ref, wv_ref, wg_ref)):
            w_scr[:, n * width : (n + 1) * width] = ref[...]
        ggain_ref[...] = jnp.zeros_like(ggain_ref)
        gw_ref[...] = jnp.zeros_like(gw_ref)

    gain = gain_ref[...]
    normed, inv_std, hidden = layer_norm(atoms_ref[0].astype(F32), gain)
    d_scr[:, :width] = dq_ref[0]
    d_scr[:, width : 3 * width] = dkv_ref[0]
    d_scr[:, 3 * width :] = dg_ref[0]
    d_scr[:rim, width : 3 * width] = (
        dkv_ref[0, :rim].astype(F32) + low_ref[0].astype(F32)
    ).astype(BF16)
    d_scr[rows - rim :, width : 3 * width] = (
        dkv_ref[0, rows - rim :].astype(F32) + high_ref[0].astype(F32)
    ).astype(BF16)
    d = d_scr[...]
    gw_ref[...] += mm(hidden, d, TN)
    grad_hidden = mm(d, w_scr[...], NT)
    gn = grad_hidden * normed
    ggain_ref[...] += jnp.sum(gn, axis=0, keepdims=True)
    gx = grad_hidden * gain
    grad_ln = inv_std * (
        gx
        - jnp.mean(gx, axis=-1, keepdims=True)
        - normed * jnp.mean(gn * gain, axis=-1, keepdims=True)
    )
    gatoms_ref[0] = (gupd_ref[0].astype(F32) + grad_ln).astype(BF16)


def axis_bits():
    bits = []
    for axis in ("samp", "seq"):
        bit = 1
        while bit < lax.axis_size(axis):
            bits.append((axis, bit))
            bit *= 2
    return bits


def sum_kernel(parts, streams, *refs):
    grads = refs[: 5 * parts]
    out_ref, buf, send_sem, recv_sem = refs[5 * parts : 5 * parts + 4]
    slots = refs[5 * parts + 4 :]

    def total(n, *at):
        value = grads[n][at] if at else grads[n][...]
        for p in range(1, parts):
            more = grads[5 * p + n]
            value = value + (more[at] if at else more[...])
        return value

    gtok_ref, rsum_ref = grads[1], grads[3]
    width = grads[0].shape[0]
    bits = axis_bits()
    count = len(bits)
    sends, recvs = slots[: streams * count], slots[streams * count :]
    where = []
    for axis, bit in bits:
        me = lax.axis_index(axis)
        upper = lax.rem(me // bit, 2)
        where.append((upper, {axis: me + bit - 2 * bit * upper}))
    barrier = pltpu.get_barrier_semaphore()
    for _, partner in where:
        pl.semaphore_signal(
            barrier, inc=1, device_id=partner, device_id_type=pl.DeviceIdType.MESH
        )

    every = slice(None)
    blocks = gtok_ref.shape[1] // width
    for n in range(blocks):
        buf[n * width : (n + 1) * width, :] = total(1, every, slice(n * width, (n + 1) * width))
    for n in range(4):
        at = (blocks + n) * width
        buf[at : at + width, :] = total(2, every, slice(n * width, (n + 1) * width))
    at = (blocks + 4) * width
    buf[at : at + width, :] = total(0)
    at += width
    buf[at:, :] = jnp.zeros((buf.shape[0] - at, width), F32)
    high, wide = rsum_ref.shape
    per = high // HEADS
    row = lax.broadcasted_iota(jnp.int32, (high, wide), 0)
    lane = lax.broadcasted_iota(jnp.int32, (high, wide), 1)
    diagonal = jnp.where(lax.rem(row, per) == lane // (wide // per), total(3), 0.0)
    for h in range(HEADS):
        line = jnp.sum(diagonal[h * per : (h + 1) * per], axis=0, keepdims=True)
        for n in range(wide // width):
            buf[at + n * HEADS + h : at + n * HEADS + h + 1, :] = line[
                :, n * width : (n + 1) * width
            ]
    spot = at + HEADS * (wide // width)
    buf[spot : spot + 1, :] = total(4)
    pl.semaphore_wait(barrier, count)

    size = buf.shape[0] // streams
    orders = []
    for stream in range(streams):
        order = list(range(count))
        turn = (stream * 2) % 3
        order[:3] = order[turn:3] + order[:turn]
        orders.append(order)
    offs = [stream * size for stream in range(streams)]
    lengths = [size] * streams
    pending = [None] * streams

    def send(stream, src, dst, slot, partner):
        copy = pltpu.make_async_remote_copy(
            src_ref=src,
            dst_ref=dst,
            send_sem=send_sem.at[stream * 2 * count + slot],
            recv_sem=recv_sem.at[stream * 2 * count + slot],
            device_id=partner,
            device_id_type=pl.DeviceIdType.MESH,
        )
        copy.start()
        pending[stream] = copy

    def absorb(stream, k):
        pending[stream].wait()
        rows = pl.ds(offs[stream], lengths[stream])
        buf[rows, :] = buf[rows, :] + recvs[stream * count + k][...].astype(F32)

    for k in range(count):
        for stream in range(streams):
            if k > 0:
                absorb(stream, k - 1)
            upper, partner = where[orders[stream][k]]
            lengths[stream] //= 2
            length = lengths[stream]
            keep = pl.multiple_of(offs[stream] + upper * length, 16)
            give = pl.multiple_of(offs[stream] + (1 - upper) * length, 16)
            slot = sends[stream * count + k]
            slot[...] = buf[pl.ds(give, length), :].astype(BF16)
            send(stream, slot, recvs[stream * count + k], k, partner)
            offs[stream] = keep
    for k in range(count - 1, -1, -1):
        for stream in range(streams):
            upper, partner = where[orders[stream][k]]
            length = lengths[stream]
            if k == count - 1:
                absorb(stream, k)
                rows = pl.ds(offs[stream], length)
                out_ref[rows, :] = buf[rows, :].astype(BF16)
            else:
                pending[stream].wait()
            part = out_ref.at[pl.ds(pl.multiple_of(offs[stream], 16), length), :]
            send(stream, part, part, count + k, partner)
            offs[stream] = offs[stream] - upper * length
            lengths[stream] *= 2
    for stream in range(streams):
        pending[stream].wait()


def unpack_kernel(packed_ref, gq_out, gk_out, gv_out, gg_out, gout_out, gtok_out, small_out):
    width = gout_out.shape[0]
    blocks = gtok_out.shape[1] // width

    def block(n):
        return packed_ref[n * width : (n + 1) * width, :].astype(F32)

    for n in range(blocks):
        gtok_out[:, n * width : (n + 1) * width] = block(n)
    for n, ref in enumerate((gq_out, gk_out, gv_out, gg_out, gout_out)):
        ref[...] = block(blocks + n)
    at = (blocks + 5) * width
    small_out[...] = packed_ref[at : at + small_out.shape[0], :].astype(F32)


def sum_all(halves):
    shape = jax.ShapeDtypeStruct
    gout, gtok, gw = halves[0][:3]
    width = gout.shape[0]
    count = len(axis_bits())
    unit = 16 * 2**count
    lines = gtok.shape[1] + gw.shape[1] + width + 16
    total = -(-lines // unit) * unit
    streams = total // unit
    slots = [pltpu.VMEM((unit >> (k + 1), width), BF16) for k in range(count)]
    operands = [x for half in halves for x in half]
    vmem = pl.BlockSpec(memory_space=pltpu.VMEM)
    packed = pl.pallas_call(
        functools.partial(sum_kernel, len(halves), streams),
        in_specs=[vmem] * len(operands),
        out_specs=vmem,
        out_shape=shape((total, width), BF16),
        scratch_shapes=[
            pltpu.VMEM((total, width), F32),
            pltpu.SemaphoreType.DMA((2 * streams * count,)),
            pltpu.SemaphoreType.DMA((2 * streams * count,)),
        ]
        + slots * (2 * streams),
        compiler_params=pltpu.CompilerParams(collective_id=0, has_side_effects=True),
    )(*operands)
    return pl.pallas_call(
        unpack_kernel,
        in_specs=[vmem],
        out_specs=[vmem] * 7,
        out_shape=[shape((width, width), F32)] * 5
        + [shape(gtok.shape, F32), shape((16, width), F32)],
    )(packed)


def per_sample(*shape, base=0):
    return pl.BlockSpec((1,) + shape, lambda s: (s + base,) + (0,) * len(shape))


def dropping(kernel, position):
    def body(*refs):
        return kernel(*refs[:position], *refs[position + 1 :])

    return body


def whole(*shape):
    return pl.BlockSpec(shape, lambda s: (0,) * len(shape))


def shifted(block, axis, distance):
    devices = range(lax.axis_size(axis))
    route = [(i - distance, i) for i in devices if i - distance in devices]
    return lax.ppermute(block, axis, route)


def on_device(
    atoms,
    gain,
    w_query,
    w_key,
    w_value,
    w_gate,
    w_out,
    w_token,
    w_pair,
    pair_cond,
    counts,
    membership,
    pooled_cot,
):
    samples, rows, width = atoms.shape
    blocks = rows // QBLK
    rim = (KWIN - QBLK) // 2
    tokens, token_width = pooled_cot.shape[1:]
    channels = w_pair.shape[0]
    per = 2 * LANES // channels
    wsm = (
        w_pair.T[:, None, None, :] * jnp.eye(per, dtype=BF16)[None, :, :, None]
    ).reshape(HEADS * per, per * channels)
    pair2 = pair_cond.reshape(blocks * QBLK, pair_cond.shape[-1])
    gain2 = gain.reshape(1, width)
    ids2 = membership.reshape(1, rows)
    square = whole(width, width)
    params = pltpu.CompilerParams(
        dimension_semantics=("arbitrary",), vmem_limit_bytes=56 * 1024 * 1024
    )
    shape = jax.ShapeDtypeStruct
    anywhere = pl.BlockSpec(memory_space=pl.ANY)

    def run_main(base, count, low, high, before):
        specs = [
            pl.BlockSpec(memory_space=pltpu.SMEM),
            per_sample(rows, width, base=base),
            per_sample(rim, width),
            per_sample(rim, width),
            whole(1, width),
            square,
            square,
            square,
            square,
            square,
            whole(width, token_width),
            whole(*wsm.shape),
            whole(*pair2.shape),
            whole(1, rows),
            per_sample(tokens, token_width, base=base),
        ]
        operands = [
            counts,
            atoms,
            low,
            high,
            gain2,
            w_query,
            w_key,
            w_value,
            w_gate,
            w_out,
            w_token,
            wsm,
            pair2,
            ids2,
            pooled_cot,
        ]
        place = len(operands)
        return pl.pallas_call(
            main_kernel if before is None else dropping(main_kernel, place),
            grid=(count,),
            in_specs=specs + ([] if before is None else [anywhere]),
            out_specs=[
                per_sample(tokens, token_width, base=base),
                per_sample(rows, width),
                per_sample(rows, width),
                per_sample(rows, 2 * width),
                per_sample(rim, 2 * width),
                per_sample(rim, 2 * width),
                per_sample(rows, width),
                square,
                whole(width, token_width),
                whole(*wsm.shape),
            ],
            out_shape=[
                shape((samples, tokens, token_width), BF16),
                shape((count, rows, width), BF16),
                shape((count, rows, width), BF16),
                shape((count, rows, 2 * width), BF16),
                shape((count, rim, 2 * width), BF16),
                shape((count, rim, 2 * width), BF16),
                shape((count, rows, width), BF16),
                shape((width, width), F32),
                shape((width, token_width), F32),
                shape(wsm.shape, F32),
            ],
            scratch_shapes=[
                pltpu.VMEM((blocks, KWIN, LANES), F32),
                pltpu.VMEM((blocks, KWIN, LANES), F32),
                pltpu.VMEM((rows, tokens), BF16),
                pltpu.VMEM((tokens, rows), BF16),
                pltpu.VMEM((tokens, 1), F32),
                pltpu.VMEM((width, 2 * width), BF16),
                pltpu.VMEM((width, 2 * width), BF16),
                pltpu.VMEM((rows + 2 * rim, width), BF16),
                pltpu.VMEM((rows, width), BF16),
                pltpu.VMEM((rows, width), F32),
                pltpu.VMEM((rows + 2 * rim, 2 * width), BF16),
                pltpu.VMEM((blocks, KWIN, LANES), F32),
                pltpu.VMEM((blocks, KWIN, LANES), BF16),
                pltpu.VMEM((rows, width), F32),
                pltpu.VMEM((rows, width), BF16),
                pltpu.VMEM((rows + 2 * rim, 2 * width), F32),
            ],
            input_output_aliases={} if before is None else {place: 0},
            cost_estimate=pl.CostEstimate(
                flops=count * rows * 4000000, bytes_accessed=1 << 22, transcendentals=0
            ),
            compiler_params=params,
        )(*operands, *([] if before is None else [before]))

    def run_tail(base, count, gupd, dq, dkv, from_left, from_right, dg, before):
        operands = [
            atoms,
            gain2,
            w_query,
            w_key,
            w_value,
            w_gate,
            gupd,
            dq,
            dkv,
            from_left,
            from_right,
            dg,
        ]
        place = len(operands)
        return pl.pallas_call(
            tail_kernel if before is None else dropping(tail_kernel, place),
            grid=(count,),
            in_specs=[
                per_sample(rows, width, base=base),
                whole(1, width),
                square,
                square,
                square,
                square,
                per_sample(rows, width),
                per_sample(rows, width),
                per_sample(rows, 2 * width),
                per_sample(rim, 2 * width),
                per_sample(rim, 2 * width),
                per_sample(rows, width),
            ]
            + ([] if before is None else [anywhere]),
            out_specs=[
                per_sample(rows, width, base=base),
                whole(1, width),
                whole(width, 4 * width),
            ],
            out_shape=[
                shape((samples, rows, width), BF16),
                shape((1, width), F32),
                shape((width, 4 * width), F32),
            ],
            scratch_shapes=[
                pltpu.VMEM((rows, 4 * width), BF16),
                pltpu.VMEM((width, 4 * width), BF16),
            ],
            input_output_aliases={} if before is None else {place: 0},
            cost_estimate=pl.CostEstimate(
                flops=count * rows * 800000, bytes_accessed=1 << 22, transcendentals=0
            ),
            compiler_params=params,
        )(*operands, *([] if before is None else [before]))

    first = samples // 2
    cuts = [(0, first), (first, samples - first)]
    rims = []
    for base, count in cuts:
        low = shifted(atoms[base : base + count, rows - rim :], "seq", 1)
        high = shifted(atoms[base : base + count, :rim], "seq", -1)
        rims.append((low, high))
    pooled = None
    mains = []
    for (base, count), (low, high) in zip(cuts, rims):
        outs = run_main(base, count, low, high, pooled)
        pooled = outs[0]
        _, gupd, dq, dkv, edge_low, edge_high, dg, gout, gtok, rsum = outs
        from_left = shifted(edge_high, "seq", 1)
        from_right = shifted(edge_low, "seq", -1)
        mains.append((gupd, dq, dkv, from_left, from_right, dg, gout, gtok, rsum))
    grad_atoms = None
    sums = []
    for (base, count), (*moved, gout, gtok, rsum) in zip(cuts, mains):
        grad_atoms, ggain, gw = run_tail(base, count, *moved, grad_atoms)
        sums.append((gout, gtok, gw, rsum, ggain))
    gq, gk, gv, gg, gout, gtok, small = sum_all(sums)
    halves = rsum.shape[1] // width
    lines = small[: halves * HEADS].reshape(halves, HEADS, width // channels, channels)
    gpair = jnp.sum(lines, axis=(0, 2)).T
    ggain = small[halves * HEADS]
    return (pooled, grad_atoms, ggain, gq, gk, gv, gg, gout, gtok, gpair)


def solution(mesh):
    placed = (
        P("samp", "seq", None),
        P(),
        P(),
        P(),
        P(),
        P(),
        P(),
        P(),
        P(),
        P("seq", None, None),
        P(),
        P("seq"),
        P("samp", "seq", None),
    )
    return jax.shard_map(
        on_device,
        mesh=mesh,
        in_specs=placed,
        out_specs=(
            P("samp", "seq", None),
            P("samp", "seq", None),
            P(),
            P(),
            P(),
            P(),
            P(),
            P(),
            P(),
            P(),
        ),
        check_vma=False,
    )
```

```python
import functools

import jax
import jax.numpy as jnp
from jax import lax
from jax.experimental import pallas as pl
from jax.experimental.pallas import tpu as pltpu
from jax.sharding import PartitionSpec as P

HEADS = 4
QBLK = 32
KWIN = 128
LOG2E = 1.4426950408889634

epsilon = 1e-05
F32 = jnp.float32
BF16 = jnp.bfloat16
NN = (((1,), (0,)), ((), ()))
NT = (((1,), (1,)), ((), ()))
TN = (((0,), (0,)), ((), ()))
GROUP = 4
LANES = 128


def mm(a, b, dims=NN):
    return lax.dot_general(a, b, dims, preferred_element_type=F32)


def sigmoid(x):
    return 0.5 * jnp.tanh(0.5 * x) + 0.5


def layer_norm(x, gain):
    centred = x - jnp.mean(x, axis=-1, keepdims=True)
    variance = jnp.mean(centred * centred, axis=-1, keepdims=True)
    inv_std = lax.rsqrt(variance + epsilon)
    normed = centred * inv_std
    return normed, inv_std, (normed * gain).astype(BF16)


def head_lanes(width):
    lane = lax.broadcasted_iota(jnp.int32, (1, width), 1)
    return lane // (width // HEADS)


def expand(block, masks):
    return jnp.concatenate([block * m for m in masks], axis=0)


def collapse(wide, lane_head):
    rows = wide.shape[0] // HEADS
    out = wide[:rows]
    for h in range(1, HEADS):
        out = jnp.where(lane_head == h, wide[h * rows : (h + 1) * rows], out)
    return out


def lane_swap(parts, lane_block):
    count = len(parts)
    outs = []
    for b in range(count):
        out = None
        for a in range(count):
            shift = (QBLK * (a - b)) % LANES
            moved = parts[a] if shift == 0 else pltpu.roll(parts[a], shift, 1)
            out = moved if out is None else jnp.where(lane_block == a, moved, out)
        outs.append(out)
    return outs


def build_bias(counts_ref, pair_ref, wsm_ref, bias_scr, blocks, rows):
    pos = lax.axis_index("seq")
    size = lax.axis_size("seq")
    own = counts_ref[pos]
    left = jnp.where(pos > 0, counts_ref[jnp.maximum(pos - 1, 0)], 0)
    right = jnp.where(pos < size - 1, counts_ref[jnp.minimum(pos + 1, size - 1)], 0)
    rim = (KWIN - QBLK) // 2
    lane_block = head_lanes(LANES)
    chunk = wsm_ref.shape[1]
    per = wsm_ref.shape[0] // HEADS
    wsm = wsm_ref[...]
    for kk in range(pair_ref.shape[1] // chunk):
        biased = mm(wsm, pair_ref[:, kk * chunk : (kk + 1) * chunk], NT)
        for g in range(blocks // GROUP):
            parts = [
                biased[h * per : (h + 1) * per, g * LANES : (g + 1) * LANES] for h in range(HEADS)
            ]
            for w, out in enumerate(lane_swap(parts, lane_block)):
                b = g * GROUP + w
                slot = (
                    lax.broadcasted_iota(jnp.int32, (per, LANES), 0) + kk * per + b * QBLK - rim
                )
                alive = (
                    ((slot < 0) & (slot + rows < left))
                    | ((slot >= 0) & (slot < own))
                    | ((slot >= rows) & (slot - rows < right))
                )
                bias_scr[b, kk * per : (kk + 1) * per, :] = jnp.where(alive, out * LOG2E, -1e30)


def pair_gradient(pair_ref, score_scr, rsum_ref, blocks):
    lane_block = head_lanes(LANES)
    per = rsum_ref.shape[0] // HEADS
    chunk = rsum_ref.shape[1]
    total = None
    for kk in range(pair_ref.shape[1] // chunk):
        columns = []
        for g in range(blocks // GROUP):
            parts = [score_scr[g * GROUP + w, kk * per : (kk + 1) * per, :] for w in range(GROUP)]
            columns.append(jnp.concatenate(lane_swap(parts, lane_block), axis=0))
        grads = jnp.concatenate(columns, axis=1).astype(BF16)
        part = mm(grads, pair_ref[:, kk * chunk : (kk + 1) * chunk])
        total = part if total is None else total + part
    rsum_ref[...] = total


def main_kernel(
    counts_ref,
    atoms_ref,
    low_ref,
    high_ref,
    gain_ref,
    wq_ref,
    wk_ref,
    wv_ref,
    wg_ref,
    wo_ref,
    wt_ref,
    wsm_ref,
    pair_ref,
    ids_ref,
    cot_ref,
    pooled_ref,
    gupd_ref,
    dq_ref,
    dkv_ref,
    edge_low_ref,
    edge_high_ref,
    dg_ref,
    gout_ref,
    gtok_ref,
    rsum_ref,
    bias_scr,
    score_scr,
    member_scr,
    member_t_scr,
    inv_scr,
    wqg_scr,
    wkv_scr,
    hid_scr,
    q_scr,
    gate_scr,
    kv_scr,
    p_scr,
    plow_scr,
    att_scr,
    gatt_scr,
    acc_scr,
):
    step = pl.program_id(0)
    rows, width = q_scr.shape
    blocks = rows // QBLK
    rim = (KWIN - QBLK) // 2
    tokens = inv_scr.shape[0]
    scaling = (width // HEADS) ** (-0.5)
    lane_head = head_lanes(width)
    masks = [(lane_head == h).astype(F32).astype(BF16) for h in range(HEADS)]

    @pl.when(step == 0)
    def _():
        pos = lax.axis_index("seq")
        build_bias(counts_ref, pair_ref, wsm_ref, bias_scr, blocks, rows)
        token = lax.broadcasted_iota(jnp.int32, (tokens, rows), 0)
        slot = lax.broadcasted_iota(jnp.int32, (tokens, rows), 1)
        hit = (ids_ref[...] - pos * tokens == token) & (slot < counts_ref[pos])
        member_t = jnp.where(hit, 1.0, 0.0).astype(F32)
        inv_scr[...] = 1.0 / jnp.sum(member_t, axis=1, keepdims=True)
        member_t_scr[...] = member_t.astype(BF16)
        member_scr[...] = member_t.T.astype(BF16)
        wqg_scr[:, :width] = wq_ref[...]
        wqg_scr[:, width:] = wg_ref[...]
        wkv_scr[:, :width] = wk_ref[...]
        wkv_scr[:, width:] = wv_ref[...]
        score_scr[...] = jnp.zeros_like(score_scr)
        gout_ref[...] = jnp.zeros_like(gout_ref)
        gtok_ref[...] = jnp.zeros_like(gtok_ref)

    gain = gain_ref[...]
    x = atoms_ref[0].astype(F32)
    hid_scr[:rim] = layer_norm(low_ref[0].astype(F32), gain)[2]
    hid_scr[rim : rim + rows] = layer_norm(x, gain)[2]
    hid_scr[rim + rows :] = layer_norm(high_ref[0].astype(F32), gain)[2]
    kv_scr[...] = mm(hid_scr[...], wkv_scr[...]).astype(BF16)
    qg = mm(hid_scr[rim : rim + rows], wqg_scr[...])
    q_scr[...] = qg[:, :width].astype(BF16)
    gate_scr[...] = sigmoid(qg[:, width:])

    for g in range(blocks // GROUP):
        spans = [g * GROUP + w for w in range(GROUP)]
        q_exp = [expand(q_scr[b * QBLK : (b + 1) * QBLK, :], masks) for b in spans]
        scores = [
            mm(kv_scr[b * QBLK : b * QBLK + KWIN, :width], q, NT) for b, q in zip(spans, q_exp)
        ]
        es = [
            jnp.exp2(sc * (scaling * LOG2E) + bias_scr[b]) for b, sc in zip(spans, scores)
        ]
        invs = [1.0 / jnp.sum(e, axis=0, keepdims=True) for e in es]
        ps = [e * inv for e, inv in zip(es, invs)]
        lows = [p.astype(BF16) for p in ps]
        for b, p, low in zip(spans, ps, lows):
            p_scr[b] = p
            plow_scr[b] = low
        wide = [
            mm(low, kv_scr[b * QBLK : b * QBLK + KWIN, width:], TN)
            for b, low in zip(spans, lows)
        ]
        for b, o in zip(spans, wide):
            att_scr[b * QBLK : (b + 1) * QBLK, :] = collapse(o, lane_head)

    gate = gate_scr[...]
    att = att_scr[...]
    gated = (gate * att).astype(BF16)
    updated = (x + mm(gated, wo_ref[...])).astype(BF16)
    chunk = 256
    half = rows // 2
    scaled_cot = (cot_ref[0].astype(F32) * inv_scr[...]).astype(BF16)
    gupd = [None, None]
    for c in range(wt_ref.shape[1] // chunk):
        cols = slice(c * chunk, (c + 1) * chunk)
        wt = wt_ref[:, cols]
        pooled = None
        gtok = None
        for r in range(2):
            span = slice(r * half, (r + 1) * half)
            pre = mm(updated[span], wt)
            sig = sigmoid(pre)
            act = pre * sig
            grad_act = mm(member_scr[span, :], scaled_cot[:, cols])
            grad_pre = (grad_act * (sig + act * (1.0 - sig))).astype(BF16)
            part = mm(member_t_scr[:, span], act.astype(BF16))
            pooled = part if pooled is None else pooled + part
            part = mm(updated[span], grad_pre, TN)
            gtok = part if gtok is None else gtok + part
            part = mm(grad_pre, wt, NT)
            gupd[r] = part if gupd[r] is None else gupd[r] + part
        pooled_ref[0, :, cols] = (pooled * inv_scr[...]).astype(BF16)
        gtok_ref[:, cols] += gtok
    grad_updated = jnp.concatenate(gupd, axis=0).astype(BF16)
    gupd_ref[0] = grad_updated
    gout_ref[...] += mm(gated, grad_updated, TN)
    grad_gate = mm(grad_updated, wo_ref[...], NT) * gate
    gatt_scr[...] = grad_gate.astype(BF16)
    dg_ref[0] = (grad_gate * att * (1.0 - gate)).astype(BF16)

    def tiles(x):
        return [x[n * QBLK : (n + 1) * QBLK] for n in range(KWIN // QBLK)]

    open_k = []
    open_v = []

    def close(first, count):
        for n in range(count):
            at = (first + n) * QBLK
            acc_scr[at : at + QBLK, :width] = open_k[n] * scaling
            acc_scr[at : at + QBLK, width:] = open_v[n]
        del open_k[:count]
        del open_v[:count]

    def merge(opened, parts):
        for n, part in enumerate(parts):
            if n < len(opened):
                opened[n] = opened[n] + part
            else:
                opened.append(part)

    for g in range(blocks // GROUP):
        spans = [g * GROUP + w for w in range(GROUP)]
        g_exp = [expand(gatt_scr[b * QBLK : (b + 1) * QBLK, :], masks) for b in spans]
        gps = [
            mm(kv_scr[b * QBLK : b * QBLK + KWIN, width:], ge, NT) for b, ge in zip(spans, g_exp)
        ]
        dvs = [mm(plow_scr[b], ge) for b, ge in zip(spans, g_exp)]
        ts = [p_scr[b] * gp for b, gp in zip(spans, gps)]
        sums = [jnp.sum(t, axis=0, keepdims=True) for t in ts]
        dss = [t - p_scr[b] * r for b, t, r in zip(spans, ts, sums)]
        lows = [ds.astype(BF16) for ds in dss]
        for b, ds in zip(spans, dss):
            score_scr[b] += ds
        q_exp = [expand(q_scr[b * QBLK : (b + 1) * QBLK, :], masks) for b in spans]
        dks = [mm(low, q) for low, q in zip(lows, q_exp)]
        dqs = [
            mm(low, kv_scr[b * QBLK : b * QBLK + KWIN, :width], TN)
            for b, low in zip(spans, lows)
        ]
        for b, dk, dv in zip(spans, dks, dvs):
            merge(open_k, tiles(dk))
            merge(open_v, tiles(dv))
            close(b, 1)
        for b, dq in zip(spans, dqs):
            dq_ref[0, b * QBLK : (b + 1) * QBLK, :] = (
                collapse(dq, lane_head) * scaling
            ).astype(BF16)
    close(blocks, len(open_k))
    edge_low_ref[0] = acc_scr[:rim].astype(BF16)
    edge_high_ref[0] = acc_scr[rim + rows :].astype(BF16)
    dkv_ref[0] = acc_scr[rim : rim + rows].astype(BF16)

    @pl.when(step == pl.num_programs(0) - 1)
    def _():
        pair_gradient(pair_ref, score_scr, rsum_ref, blocks)


def tail_kernel(
    atoms_ref,
    gain_ref,
    wq_ref,
    wk_ref,
    wv_ref,
    wg_ref,
    gupd_ref,
    dq_ref,
    dkv_ref,
    low_ref,
    high_ref,
    dg_ref,
    gatoms_ref,
    ggain_ref,
    gw_ref,
    d_scr,
    w_scr,
):
    step = pl.program_id(0)
    rows, width = atoms_ref.shape[1:]
    rim = low_ref.shape[1]

    @pl.when(step == 0)
    def _():
        for n, ref in enumerate((wq_ref, wk_ref, wv_ref, wg_ref)):
            w_scr[:, n * width : (n + 1) * width] = ref[...]
        ggain_ref[...] = jnp.zeros_like(ggain_ref)
        gw_ref[...] = jnp.zeros_like(gw_ref)

    gain = gain_ref[...]
    normed, inv_std, hidden = layer_norm(atoms_ref[0].astype(F32), gain)
    d_scr[:, :width] = dq_ref[0]
    d_scr[:, width : 3 * width] = dkv_ref[0]
    d_scr[:, 3 * width :] = dg_ref[0]
    d_scr[:rim, width : 3 * width] = (
        dkv_ref[0, :rim].astype(F32) + low_ref[0].astype(F32)
    ).astype(BF16)
    d_scr[rows - rim :, width : 3 * width] = (
        dkv_ref[0, rows - rim :].astype(F32) + high_ref[0].astype(F32)
    ).astype(BF16)
    d = d_scr[...]
    gw_ref[...] += mm(hidden, d, TN)
    grad_hidden = mm(d, w_scr[...], NT)
    gn = grad_hidden * normed
    ggain_ref[...] += jnp.sum(gn, axis=0, keepdims=True)
    gx = grad_hidden * gain
    grad_ln = inv_std * (
        gx
        - jnp.mean(gx, axis=-1, keepdims=True)
        - normed * jnp.mean(gn * gain, axis=-1, keepdims=True)
    )
    gatoms_ref[0] = (gupd_ref[0].astype(F32) + grad_ln).astype(BF16)


def axis_sizes():
    return [(axis, lax.axis_size(axis)) for axis in ("samp", "seq")]


def sum_kernel(parts, streams, *refs):
    grads = refs[: 5 * parts]
    out_ref, buf, send_sem, recv_sem = refs[5 * parts : 5 * parts + 4]
    slots = refs[5 * parts + 4 :]

    def total(n, *at):
        value = grads[n][at] if at else grads[n][...]
        for p in range(1, parts):
            more = grads[5 * p + n]
            value = value + (more[at] if at else more[...])
        return value

    gtok_ref, rsum_ref = grads[1], grads[3]
    width = grads[0].shape[0]
    axes = axis_sizes()
    peers = sum(size - 1 for _, size in axes)
    sends, recvs = slots[: 2 * streams], slots[2 * streams :]

    def peer(axis, size, distance):
        return lax.rem(lax.axis_index(axis) + distance, size)

    barrier = pltpu.get_barrier_semaphore()
    for axis, size in axes:
        for d in range(1, size):
            pl.semaphore_signal(
                barrier,
                inc=1,
                device_id={axis: peer(axis, size, d)},
                device_id_type=pl.DeviceIdType.MESH,
            )

    every = slice(None)
    blocks = gtok_ref.shape[1] // width
    for n in range(blocks):
        buf[n * width : (n + 1) * width, :] = total(1, every, slice(n * width, (n + 1) * width))
    for n in range(4):
        at = (blocks + n) * width
        buf[at : at + width, :] = total(2, every, slice(n * width, (n + 1) * width))
    at = (blocks + 4) * width
    buf[at : at + width, :] = total(0)
    at += width
    buf[at:, :] = jnp.zeros((buf.shape[0] - at, width), F32)
    high, wide = rsum_ref.shape
    per = high // HEADS
    row = lax.broadcasted_iota(jnp.int32, (high, wide), 0)
    lane = lax.broadcasted_iota(jnp.int32, (high, wide), 1)
    diagonal = jnp.where(lax.rem(row, per) == lane // (wide // per), total(3), 0.0)
    for h in range(HEADS):
        line = jnp.sum(diagonal[h * per : (h + 1) * per], axis=0, keepdims=True)
        for n in range(wide // width):
            buf[at + n * HEADS + h : at + n * HEADS + h + 1, :] = line[
                :, n * width : (n + 1) * width
            ]
    spot = at + HEADS * (wide // width)
    buf[spot : spot + 1, :] = total(4)
    pl.semaphore_wait(barrier, peers)

    unit = buf.shape[0] // streams
    orders = [axes[::-1] if stream % 3 == 1 else axes for stream in range(streams)]
    offs = [stream * unit for stream in range(streams)]
    lengths = [unit] * streams
    pending = [[] for _ in range(streams)]

    def send(stream, src, dst, slot, partner):
        copy = pltpu.make_async_remote_copy(
            src_ref=src,
            dst_ref=dst,
            send_sem=send_sem.at[stream * 2 * peers + slot],
            recv_sem=recv_sem.at[stream * 2 * peers + slot],
            device_id=partner,
            device_id_type=pl.DeviceIdType.MESH,
        )
        copy.start()
        pending[stream].append(copy)

    def absorb(stream, k):
        rows = pl.ds(pl.multiple_of(offs[stream], 16), lengths[stream])
        value = buf[rows, :]
        for n, copy in enumerate(pending[stream]):
            copy.wait()
            value = value + recvs[2 * stream + k][n].astype(F32)
        pending[stream] = []
        return rows, value

    for k in range(2):
        for stream in range(streams):
            axis, size = orders[stream][k]
            base = 0
            if k > 0:
                rows, value = absorb(stream, k - 1)
                buf[rows, :] = value
                base = orders[stream][0][1] - 1
            length = lengths[stream] // size
            for d in range(1, size):
                to = peer(axis, size, d)
                give = pl.multiple_of(offs[stream] + to * length, 16)
                slot = sends[2 * stream + k].at[d - 1]
                slot[...] = buf[pl.ds(give, length), :].astype(BF16)
                send(stream, slot, recvs[2 * stream + k].at[d - 1], base + d - 1, {axis: to})
            lengths[stream] = length
            offs[stream] = offs[stream] + lax.axis_index(axis) * length
    for k in (1, 0):
        for stream in range(streams):
            axis, size = orders[stream][k]
            base = peers
            if k == 1:
                rows, value = absorb(stream, 1)
                out_ref[rows, :] = value.astype(BF16)
            else:
                for copy in pending[stream]:
                    copy.wait()
                pending[stream] = []
                base += orders[stream][1][1] - 1
            length = lengths[stream]
            part = out_ref.at[pl.ds(pl.multiple_of(offs[stream], 16), length), :]
            for d in range(1, size):
                send(stream, part, part, base + d - 1, {axis: peer(axis, size, d)})
            offs[stream] = offs[stream] - lax.axis_index(axis) * length
            lengths[stream] = length * size
    for stream in range(streams):
        for copy in pending[stream]:
            copy.wait()


def unpack_kernel(packed_ref, gq_out, gk_out, gv_out, gg_out, gout_out, gtok_out, small_out):
    width = gout_out.shape[0]
    blocks = gtok_out.shape[1] // width

    def block(n):
        return packed_ref[n * width : (n + 1) * width, :].astype(F32)

    for n in range(blocks):
        gtok_out[:, n * width : (n + 1) * width] = block(n)
    for n, ref in enumerate((gq_out, gk_out, gv_out, gg_out, gout_out)):
        ref[...] = block(blocks + n)
    at = (blocks + 5) * width
    small_out[...] = packed_ref[at : at + small_out.shape[0], :].astype(F32)


def sum_all(halves):
    shape = jax.ShapeDtypeStruct
    gout, gtok, gw = halves[0][:3]
    width = gout.shape[0]
    axes = axis_sizes()
    devices = axes[0][1] * axes[1][1]
    peers = sum(size - 1 for _, size in axes)
    unit = 16 * devices
    lines = gtok.shape[1] + gw.shape[1] + width + 16
    total = -(-lines // unit) * unit
    streams = total // unit
    slots = []
    for stream in range(streams):
        length = unit
        for _, size in axes[::-1] if stream % 3 == 1 else axes:
            length //= size
            slots.append(pltpu.VMEM((size - 1, length, width), BF16))
    operands = [x for half in halves for x in half]
    vmem = pl.BlockSpec(memory_space=pltpu.VMEM)
    packed = pl.pallas_call(
        functools.partial(sum_kernel, len(halves), streams),
        in_specs=[vmem] * len(operands),
        out_specs=vmem,
        out_shape=shape((total, width), BF16),
        scratch_shapes=[
            pltpu.VMEM((total, width), F32),
            pltpu.SemaphoreType.DMA((2 * streams * peers,)),
            pltpu.SemaphoreType.DMA((2 * streams * peers,)),
        ]
        + slots * 2,
        compiler_params=pltpu.CompilerParams(collective_id=0, has_side_effects=True),
    )(*operands)
    return pl.pallas_call(
        unpack_kernel,
        in_specs=[vmem],
        out_specs=[vmem] * 7,
        out_shape=[shape((width, width), F32)] * 5
        + [shape(gtok.shape, F32), shape((16, width), F32)],
    )(packed)


def per_sample(*shape, base=0):
    return pl.BlockSpec((1,) + shape, lambda s: (s + base,) + (0,) * len(shape))


def dropping(kernel, position):
    def body(*refs):
        return kernel(*refs[:position], *refs[position + 1 :])

    return body


def whole(*shape):
    return pl.BlockSpec(shape, lambda s: (0,) * len(shape))


def shifted(block, axis, distance):
    devices = range(lax.axis_size(axis))
    route = [(i - distance, i) for i in devices if i - distance in devices]
    return lax.ppermute(block, axis, route)


def on_device(
    atoms,
    gain,
    w_query,
    w_key,
    w_value,
    w_gate,
    w_out,
    w_token,
    w_pair,
    pair_cond,
    counts,
    membership,
    pooled_cot,
):
    samples, rows, width = atoms.shape
    blocks = rows // QBLK
    rim = (KWIN - QBLK) // 2
    tokens, token_width = pooled_cot.shape[1:]
    channels = w_pair.shape[0]
    per = 2 * LANES // channels
    wsm = (
        w_pair.T[:, None, None, :] * jnp.eye(per, dtype=BF16)[None, :, :, None]
    ).reshape(HEADS * per, per * channels)
    pair2 = pair_cond.reshape(blocks * QBLK, pair_cond.shape[-1])
    gain2 = gain.reshape(1, width)
    ids2 = membership.reshape(1, rows)
    square = whole(width, width)
    params = pltpu.CompilerParams(
        dimension_semantics=("arbitrary",), vmem_limit_bytes=56 * 1024 * 1024
    )
    shape = jax.ShapeDtypeStruct
    anywhere = pl.BlockSpec(memory_space=pl.ANY)

    def run_main(base, count, low, high, before):
        specs = [
            pl.BlockSpec(memory_space=pltpu.SMEM),
            per_sample(rows, width, base=base),
            per_sample(rim, width, base=base),
            per_sample(rim, width, base=base),
            whole(1, width),
            square,
            square,
            square,
            square,
            square,
            whole(width, token_width),
            whole(*wsm.shape),
            whole(*pair2.shape),
            whole(1, rows),
            per_sample(tokens, token_width, base=base),
        ]
        operands = [
            counts,
            atoms,
            low,
            high,
            gain2,
            w_query,
            w_key,
            w_value,
            w_gate,
            w_out,
            w_token,
            wsm,
            pair2,
            ids2,
            pooled_cot,
        ]
        place = len(operands)
        return pl.pallas_call(
            main_kernel if before is None else dropping(main_kernel, place),
            grid=(count,),
            in_specs=specs + ([] if before is None else [anywhere]),
            out_specs=[
                per_sample(tokens, token_width, base=base),
                per_sample(rows, width),
                per_sample(rows, width),
                per_sample(rows, 2 * width),
                per_sample(rim, 2 * width),
                per_sample(rim, 2 * width),
                per_sample(rows, width),
                square,
                whole(width, token_width),
                whole(*wsm.shape),
            ],
            out_shape=[
                shape((samples, tokens, token_width), BF16),
                shape((count, rows, width), BF16),
                shape((count, rows, width), BF16),
                shape((count, rows, 2 * width), BF16),
                shape((count, rim, 2 * width), BF16),
                shape((count, rim, 2 * width), BF16),
                shape((count, rows, width), BF16),
                shape((width, width), F32),
                shape((width, token_width), F32),
                shape(wsm.shape, F32),
            ],
            scratch_shapes=[
                pltpu.VMEM((blocks, KWIN, LANES), F32),
                pltpu.VMEM((blocks, KWIN, LANES), F32),
                pltpu.VMEM((rows, tokens), BF16),
                pltpu.VMEM((tokens, rows), BF16),
                pltpu.VMEM((tokens, 1), F32),
                pltpu.VMEM((width, 2 * width), BF16),
                pltpu.VMEM((width, 2 * width), BF16),
                pltpu.VMEM((rows + 2 * rim, width), BF16),
                pltpu.VMEM((rows, width), BF16),
                pltpu.VMEM((rows, width), F32),
                pltpu.VMEM((rows + 2 * rim, 2 * width), BF16),
                pltpu.VMEM((blocks, KWIN, LANES), F32),
                pltpu.VMEM((blocks, KWIN, LANES), BF16),
                pltpu.VMEM((rows, width), F32),
                pltpu.VMEM((rows, width), BF16),
                pltpu.VMEM((rows + 2 * rim, 2 * width), F32),
            ],
            input_output_aliases={} if before is None else {place: 0},
            cost_estimate=pl.CostEstimate(
                flops=count * rows * 4000000, bytes_accessed=1 << 22, transcendentals=0
            ),
            compiler_params=params,
        )(*operands, *([] if before is None else [before]))

    def run_tail(base, count, gupd, dq, dkv, from_left, from_right, dg, before):
        operands = [
            atoms,
            gain2,
            w_query,
            w_key,
            w_value,
            w_gate,
            gupd,
            dq,
            dkv,
            from_left,
            from_right,
            dg,
        ]
        place = len(operands)
        return pl.pallas_call(
            tail_kernel if before is None else dropping(tail_kernel, place),
            grid=(count,),
            in_specs=[
                per_sample(rows, width, base=base),
                whole(1, width),
                square,
                square,
                square,
                square,
                per_sample(rows, width),
                per_sample(rows, width),
                per_sample(rows, 2 * width),
                per_sample(rim, 2 * width),
                per_sample(rim, 2 * width),
                per_sample(rows, width),
            ]
            + ([] if before is None else [anywhere]),
            out_specs=[
                per_sample(rows, width, base=base),
                whole(1, width),
                whole(width, 4 * width),
            ],
            out_shape=[
                shape((samples, rows, width), BF16),
                shape((1, width), F32),
                shape((width, 4 * width), F32),
            ],
            scratch_shapes=[
                pltpu.VMEM((rows, 4 * width), BF16),
                pltpu.VMEM((width, 4 * width), BF16),
            ],
            input_output_aliases={} if before is None else {place: 0},
            cost_estimate=pl.CostEstimate(
                flops=count * rows * 800000, bytes_accessed=1 << 22, transcendentals=0
            ),
            compiler_params=params,
        )(*operands, *([] if before is None else [before]))

    first = samples // 2
    cuts = [(0, first), (first, samples - first)]
    low = shifted(atoms[:, rows - rim :], "seq", 1)
    high = shifted(atoms[:, :rim], "seq", -1)
    pooled = None
    mains = []
    for base, count in cuts:
        outs = run_main(base, count, low, high, pooled)
        pooled = outs[0]
        _, gupd, dq, dkv, edge_low, edge_high, dg, gout, gtok, rsum = outs
        from_left = shifted(edge_high, "seq", 1)
        from_right = shifted(edge_low, "seq", -1)
        mains.append((gupd, dq, dkv, from_left, from_right, dg, gout, gtok, rsum))
    grad_atoms = None
    sums = []
    for (base, count), (*moved, gout, gtok, rsum) in zip(cuts, mains):
        grad_atoms, ggain, gw = run_tail(base, count, *moved, grad_atoms)
        sums.append((gout, gtok, gw, rsum, ggain))
    gq, gk, gv, gg, gout, gtok, small = sum_all(sums)
    halves = rsum.shape[1] // width
    lines = small[: halves * HEADS].reshape(halves, HEADS, width // channels, channels)
    gpair = jnp.sum(lines, axis=(0, 2)).T
    ggain = small[halves * HEADS]
    return (pooled, grad_atoms, ggain, gq, gk, gv, gg, gout, gtok, gpair)


def solution(mesh):
    placed = (
        P("samp", "seq", None),
        P(),
        P(),
        P(),
        P(),
        P(),
        P(),
        P(),
        P(),
        P("seq", None, None),
        P(),
        P("seq"),
        P("samp", "seq", None),
    )
    return jax.shard_map(
        on_device,
        mesh=mesh,
        in_specs=placed,
        out_specs=(
            P("samp", "seq", None),
            P("samp", "seq", None),
            P(),
            P(),
            P(),
            P(),
            P(),
            P(),
            P(),
            P(),
        ),
        check_vma=False,
    )
```
